32 devices in a mesh: tile: 8 (over z, y), band: 4 (over x, core).
Axes of the slice: x: 2, y: 2, z: 4, core: 2. Of those that a mesh axis runs over, the one named last changes fastest.
Arguments:
- background: float32 [36, 36, 8, 8, 128], P('band', None, 'tile'), may hold values from 0.2 to 2
- tangent: float32 [36, 36, 8, 8, 128], P('band', None, 'tile'), may hold values from -6 to 6
- sea_mask: int32 [8, 8, 128], P('tile'), may hold values 0 or 1
- coupling: float32 [36], P('band'), may hold values from 0.005 to 0.05
- freq_offsets: int32 [2], replicated, may hold values from 1 to 3, as said below
- dir_offsets: int32 [2], replicated, may hold values from 1 to 5
Outputs:
- background_out: float32 [36, 36, 8, 8, 128], P('band', None, 'tile')
- tangent_out: float32 [36, 36, 8, 8, 128], P('band', None, 'tile')
The draws below stay inside these ranges and needn't reach their ends.
Inputs may be any that keep to these rules, and one draw needn't show every extreme that they name: `freq_offsets`: one of the two offsets equals 3, the other is smaller.
All inputs are finite; a program needn't handle non-finite values. No bound on the sum of `sea_mask` on one device may be relied on, other than what follows from the above.
Results may differ from the reference program's by a relative error of at most 0.00002.
Values sent between devices are 32-bit elements; how exact they have to be, the bound alone decides.
No kernel may reach another device: no remote copies, remote signals or barrier semaphores. Data moves between devices by JAX's collectives and lax.ppermute only.
A program may use at most 64 MiB of HBM per device.

```python
import math
import jax
import jax.numpy as jnp
from jax import lax

NF = 36
ND = 36
CLAT = 8
CLON = 128
TY = 4
FH = 3
STEPS = 2
SUBSTEPS = 2
TILES = 8


def draw_freq_offsets(key, part):
    first_key, second_key = jax.random.split(jax.random.fold_in(key, 11), 2)
    other = jax.random.randint(first_key, (), 1, FH)
    which = jax.random.randint(second_key, (), 0, 2)
    upper = jnp.where(which == 0, FH, other)
    lower = jnp.where(which == 0, other, FH)
    return jnp.stack([upper, lower]).astype(jnp.int32)


def plant(values, rng, least, high):
    extent = values.shape
    spot = [jax.random.randint(jax.random.fold_in(rng, axis), (), 0, extent[axis]) for axis in range(len(extent))]
    values = values.at[tuple(spot)].set(least)
    longest = extent.index(max(extent))
    spot[longest] = (spot[longest] + 1) % extent[longest]
    return values.at[tuple(spot)].set(high)


def block_scale(own_key, shape, pieces, low, largest):
    loudness = 1.0
    for position, blocks in pieces:
        heights = jax.random.uniform(jax.random.fold_in(jax.random.fold_in(own_key, 6), position), (blocks,), jnp.float32, low / len(pieces), largest / len(pieces))
        loudness = loudness * jnp.repeat(jnp.exp(heights), shape[position] // blocks).reshape((-1,) + (1,) * (len(shape) - 1 - position))
    return loudness


def gaussian(key, dims, deviation, bound, shards=(), kind=jnp.bfloat16):
    drawn = deviation * jax.random.normal(key, dims, jnp.float32)
    if shards:
        drawn = drawn * block_scale(key, dims, shards, -0.22, 0.18)
    return jnp.clip(drawn, -bound, bound).astype(kind)


def setup_inputs(seed: int = 0) -> dict:
    splits = jax.random.split(jax.random.key(seed), 7)
    background = jnp.clip(jnp.exp(math.log(2.0) - 2.3025851 * jax.random.uniform(splits[0], (NF, ND, TILES, CLAT, CLON), jnp.float32) ** block_scale(splits[0], (NF, ND, TILES, CLAT, CLON), ((0, 4), (2, 8)), -0.2, 0.2)), 0.2, 2.0)
    tangent = gaussian(splits[1], (NF, ND, TILES, CLAT, CLON), 1.0, 6.0, ((0, 4), (2, 8)), jnp.float32)
    sea_mask = plant((jax.random.randint(splits[2], (TILES, CLAT, CLON), 0, 5) < 4).astype(jnp.int32), jax.random.fold_in(splits[2], 1), 0, 1)
    coupling = jnp.clip(jnp.exp(math.log(0.05) - 2.3025851 * jax.random.uniform(splits[3], (NF,), jnp.float32) ** block_scale(splits[3], (NF,), ((0, 4),), -0.2, 0.2)), 0.005, 0.05)
    freq_offsets = draw_freq_offsets(jax.random.fold_in(splits[6], 71), 0)
    dir_offsets = jax.random.randint(splits[5], (2,), 1, 6).astype(jnp.int32)
    return dict(background=background, tangent=tangent, sea_mask=sea_mask, coupling=coupling, freq_offsets=freq_offsets, dir_offsets=dir_offsets)


weight_plus = 1.0 / 1.25 ** 4
weight_minus = 1.0 / 0.75 ** 4
weight_cross = 1.0 / (1.0 - 0.25 ** 2) ** 4
source_step = 0.5


def interaction(centre, tangent_c, upper_f, upper_t, lower_f, lower_t):
    linear = weight_plus * upper_f + weight_minus * lower_f
    rate = centre * centre * linear - weight_cross * centre * upper_f * lower_f
    change = (2.0 * centre * tangent_c * linear
              + centre * centre * (weight_plus * upper_t + weight_minus * lower_t)
              - weight_cross * (tangent_c * upper_f * lower_f + centre * upper_t * lower_f + centre * upper_f * lower_t))
    return rate, change


def apply_source(centre_pair, upper_pair, lower_pair, strength, dir_one, dir_two, dir_axis):
    upper_first = jnp.roll(upper_pair, -dir_one, dir_axis)
    lower_first = jnp.roll(lower_pair, dir_two, dir_axis)
    upper_second = jnp.roll(upper_pair, dir_one, dir_axis)
    lower_second = jnp.roll(lower_pair, -dir_two, dir_axis)
    rate_one, change_one = interaction(centre_pair[0], centre_pair[1], upper_first[0], upper_first[1], lower_first[0], lower_first[1])
    rate_two, change_two = interaction(centre_pair[0], centre_pair[1], upper_second[0], upper_second[1], lower_second[0], lower_second[1])
    background = centre_pair[0] - source_step * (strength * (rate_one + rate_two))
    tangent = centre_pair[1] - source_step * (strength * (change_one + change_two))
    return jnp.stack([background, tangent])


def upwind(padded, sea_float, rate_east, rate_west, rate_north, rate_south):
    centre = padded[..., 1:-1, 1:-1]
    west = padded[..., 1:-1, :-2]
    east = padded[..., 1:-1, 2:]
    south = padded[..., :-2, 1:-1]
    north = padded[..., 2:, 1:-1]
    return sea_float * (centre - rate_east * (centre - west) + rate_west * (east - centre)
                        - rate_north * (centre - south) + rate_south * (north - centre))


def to_grid(field, tiles_lon):
    field = jnp.roll(field, TY // 2, axis=-3)
    lead = field.shape[:-3]
    shaped = field.reshape(lead + (tiles_lon, TY, CLAT, CLON))
    count = len(lead)
    order = tuple(range(count)) + (count + 1, count + 2, count, count + 3)
    return shaped.transpose(order).reshape(lead + (TY * CLAT, tiles_lon * CLON))


def from_grid(grid, tiles_lon):
    lead = grid.shape[:-2]
    shaped = grid.reshape(lead + (TY, CLAT, tiles_lon, CLON))
    count = len(lead)
    order = tuple(range(count)) + (count + 2, count, count + 1, count + 3)
    tiles = shaped.transpose(order).reshape(lead + (TY * tiles_lon, CLAT, CLON))
    return jnp.roll(tiles, -(TY // 2), axis=-3)


def reference(background, tangent, sea_mask, coupling, freq_offsets, dir_offsets):
    tiles_lon = TILES // TY
    sea_float = sea_mask.astype(jnp.float32)
    sea_grid = to_grid(sea_float, tiles_lon)
    angles = (jnp.arange(ND, dtype=jnp.float32) + 0.5) * (2.0 * jnp.pi / ND)
    fields = jnp.stack([background, tangent], 1) * sea_float

    def propagate(level, field):
        speed = 0.7 * jnp.power(jnp.float32(1.1), -level.astype(jnp.float32))
        along_x = (speed * jnp.cos(angles))[:, None, None]
        along_y = (speed * jnp.sin(angles))[:, None, None]
        rate_east = jnp.maximum(along_x, 0.0)
        rate_west = jnp.maximum(-along_x, 0.0)
        rate_north = jnp.maximum(along_y, 0.0)
        rate_south = jnp.maximum(-along_y, 0.0)
        grid = to_grid(field, tiles_lon)
        for substep in range(SUBSTEPS):
            padded = jnp.pad(grid, ((0, 0), (0, 0), (1, 1), (0, 0)))
            padded = jnp.concatenate([padded[..., -1:], padded, padded[..., :1]], axis=-1)
            grid = upwind(padded, sea_grid, rate_east, rate_west, rate_north, rate_south)
        return from_grid(grid, tiles_lon)

    for model_step in range(STEPS):
        fields = lax.map(lambda item: propagate(item[0], item[1]), (jnp.arange(NF, dtype=jnp.int32), fields))
        padded = jnp.pad(fields, ((FH, FH), (0, 0), (0, 0), (0, 0), (0, 0), (0, 0)))

        def at_level(level):
            centre = lax.dynamic_index_in_dim(fields, level, 0, False)
            upper = lax.dynamic_index_in_dim(padded, FH + level + freq_offsets[0], 0, False)
            lower = lax.dynamic_index_in_dim(padded, FH + level - freq_offsets[1], 0, False)
            strength = lax.dynamic_index_in_dim(coupling, level, 0, False)
            return apply_source(centre, upper, lower, strength, dir_offsets[0], dir_offsets[1], 1)

        fields = lax.map(at_level, jnp.arange(NF, dtype=jnp.int32))
    return fields[:, 0], fields[:, 1]
```

```python
import functools
import math

import jax
import jax.numpy as jnp
import numpy as np
from jax import lax
from jax.experimental import pallas as pl
from jax.experimental.pallas import tpu as pltpu
from jax.sharding import PartitionSpec as P

TY = 4
FH = 3
STEPS = 2

weight_plus = 1.0 / 1.25**4
weight_minus = 1.0 / 0.75**4
weight_cross = 1.0 / (1.0 - 0.25**2) ** 4
source_step = 0.5

VM = pl.BlockSpec(memory_space=pltpu.VMEM)
SM = pl.BlockSpec(memory_space=pltpu.SMEM)
f32 = jnp.float32


def rotate(x, shift, axis):
    shift = shift % x.shape[axis]
    return x if shift == 0 else pltpu.roll(x, shift, axis)


class Plan:
    def __init__(self, bins, nd, rows, lanes):
        self.bins, self.nd, self.rows, self.lanes = bins, nd, rows, lanes
        self.half, self.quad = nd // 2, nd // 4
        self.group = lanes // nd
        self.groups = -(-bins // self.group)
        self.angles = (np.arange(self.quad) + 0.5) * (2.0 * math.pi / nd)
        self.tile = (rows, lanes)

    def pairs(self):
        for i in range(self.quad):
            yield 0, i, i, self.half - 1 - i
        for i in range(self.quad):
            yield 1, i, self.nd - 1 - i, self.half + i

    def row_shape(self):
        return (self.bins * self.quad + 1,) + self.tile

    def col_shape(self):
        return (2, 2 * self.groups + 1) + self.tile

    def lane_table(self):
        table = np.zeros(self.tile, np.float32)
        for lane in range(self.group * self.nd):
            i = (lane % self.nd) // 2 % self.quad
            table[0, lane] = math.cos(self.angles[i])
            table[1, lane] = math.sin(self.angles[i])
        return table


def iotas(plan):
    sub = lax.broadcasted_iota(jnp.int32, plan.tile, 0)
    lane = lax.broadcasted_iota(jnp.int32, plan.tile, 1)
    return sub, lane


def pack(plan, f_ref, g_ref, mask, north_ref, south_ref, col_ref):
    sub, lane = iotas(plan)
    pair_lane = lane // 2
    rows, lanes = plan.tile
    north_ref[plan.bins * plan.quad] = mask
    south_ref[plan.bins * plan.quad] = mask
    col_ref[...] = jnp.zeros(col_ref.shape, f32)
    for side in range(2):
        col_ref[side, 2 * plan.groups] = mask

    def level(k, _):
        packed = [[jnp.zeros(plan.tile, f32) for _ in range(2)] for _ in range(2)]
        for sign, i, east, west in plan.pairs():
            tiles = [ref[k, j] * mask for j in (east, west) for ref in (f_ref, g_ref)]
            start = rows - 2 if sign == 0 else 0
            edge = rotate(tiles[3], 6 - start, 0)
            for n in (2, 1, 0):
                edge = jnp.where(sub < 2 * n + 2, rotate(tiles[n], 2 * n - start, 0), edge)
            (north_ref if sign == 0 else south_ref)[k * plan.quad + i] = edge
            slot = sign * plan.quad + i
            for side in range(2):
                shift = 2 * slot - (lanes - 2 if side == 0 else 0)
                for field in range(2):
                    packed[side][field] = jnp.where(
                        pair_lane == slot, rotate(tiles[2 * side + field], shift, 1), packed[side][field]
                    )
        place = lax.rem(k, plan.group)
        for side in range(2):
            for field in range(2):
                where = field * plan.groups + lax.div(k, plan.group)
                moved = pltpu.roll(packed[side][field], place * plan.nd, 1)
                col_ref[side, where] = col_ref[side, where] + moved
        return 0

    lax.fori_loop(0, plan.bins, level, 0)


def pack_kernel(plan, f_ref, g_ref, mask_ref, north_ref, south_ref, col_ref):
    pack(plan, f_ref, g_ref, mask_ref[...].astype(f32), north_ref, south_ref, col_ref)


def propagate_kernel(
    plan, speed_ref, f_ref, g_ref, mask_ref, south_ref, north_ref, col_ref, below_ref, above_ref, table_ref,
    fo_ref, go_ref, up_ref, down_ref, row_next, col_both,
):
    sub, lane = iotas(plan)
    rows, lanes = plan.tile
    bins, quad, nd, group, groups = plan.bins, plan.quad, plan.nd, plan.group, plan.groups
    mask = mask_ref[...].astype(f32)
    base = lax.axis_index("band") * bins
    last = bins * quad
    cosines = [math.cos(a) for a in plan.angles]
    sines = [math.sin(a) for a in plan.angles]
    row_masks = [
        jnp.broadcast_to(south_ref[last, rows - 1 : rows, :], plan.tile),
        jnp.broadcast_to(north_ref[last, 0:1, :], plan.tile),
    ]
    messages = [south_ref, north_ref]
    first_half = sub < rows // 2
    outer = (first_half & (lane == 0)) | (~first_half & (lane == lanes - 1))

    in_group = lane // nd
    slot = (lane % nd) // 2
    odd = lane % 2 == 1
    northward = slot < quad
    for side in range(2):
        near = jnp.broadcast_to(
            col_ref[side, 2 * groups, :, lanes - 1 : lanes] if side == 0 else col_ref[side, 2 * groups, :, 0:1],
            plan.tile,
        )
        edge_lane = 0 if side == 0 else lanes - 1
        corner_masks = [
            jnp.broadcast_to(row_masks[sign][0:1, edge_lane : edge_lane + 1], plan.tile) for sign in range(2)
        ]
        for part in range(groups):
            speeds = jnp.zeros(plan.tile, f32)
            for n in range(group):
                k = part * group + n
                if k < bins:
                    speeds = jnp.where(in_group == n, speed_ref[base + k], speeds)
            ua = speeds * jnp.broadcast_to(table_ref[0:1, :], plan.tile)
            va = speeds * jnp.broadcast_to(table_ref[1:2, :], plan.tile)
            stay = 1.0 - ua - va
            for field in range(2):
                at = field * groups + part
                here = col_ref[side, at]
                below = jnp.broadcast_to(below_ref[side, at], plan.tile)
                above = jnp.broadcast_to(above_ref[side, at], plan.tile)
                across = rotate(here, 1 if side == 0 else -1, 1)
                along = jnp.where(
                    northward,
                    jnp.where(sub == 0, below, rotate(here, 1, 0)),
                    jnp.where(sub == rows - 1, above, rotate(here, -1, 0)),
                )
                after = near * (stay * here + ua * across + va * along)
                corner = jnp.where(
                    northward & (sub == 0),
                    corner_masks[0] * below,
                    jnp.where(~northward & (sub == rows - 1), corner_masks[1] * above, 0.0),
                )
                after = after + va * corner
                if side == 0:
                    col_both[side, at] = jnp.where(odd, here, rotate(after, -1, 1))
                else:
                    col_both[side, at] = jnp.where(odd, rotate(after, 1, 1), here)

    def level(k, _):
        speed = speed_ref[base + k]
        place = lax.rem(k, group)
        back = lax.rem(lanes - place * nd, lanes)
        columns = [
            [pltpu.roll(col_both[side, field * groups + lax.div(k, group)], back, 1) for field in range(2)]
            for side in range(2)
        ]
        for sign, i, east, west in plan.pairs():
            message = messages[sign]
            u, v = speed * cosines[i], speed * sines[i]
            stay = 1.0 - u - v
            at = k * quad + i
            halo = message[at]
            across = jnp.where(first_half, rotate(halo, 1, 1), rotate(halo, -1, 1))
            across = jnp.where(outer, 0.0, across)
            along = rotate(halo, 1 if sign == 0 else -1, 0)
            row_next[at] = row_masks[sign] * (stay * halo + u * across + v * along)
            edge_row = 0 if sign == 0 else rows - 1
            step_row = 1 if sign == 0 else -1
            for side in range(2):
                j = east if side == 0 else west
                into = 1 if side == 0 else -1
                near_lane = 0 if side == 0 else lanes - 1
                far_lane = lanes - 1 - near_lane
                for field in range(2):
                    ref, out = ((f_ref, fo_ref), (g_ref, go_ref))[field]
                    inner = 4 * side + 2 * field + (1 if sign == 0 else 0)
                    slot_at = 2 * (sign * quad + i)
                    column = rotate(
                        columns[side][field], -(slot_at + 1) if side == 0 else lanes - 1 - slot_at, 1
                    )
                    x = ref[k, j] * mask
                    xu = jnp.where(lane == near_lane, column, rotate(x, into, 1))
                    xv = jnp.where(
                        sub == edge_row,
                        jnp.broadcast_to(message[at, inner : inner + 1, :], plan.tile),
                        rotate(x, step_row, 0),
                    )
                    x = mask * (stay * x + u * xu + v * xv)
                    xu = rotate(jnp.where(lane == far_lane, column, x), into, 1)
                    xv = jnp.where(
                        sub == edge_row,
                        jnp.broadcast_to(row_next[at, inner : inner + 1, :], plan.tile),
                        rotate(x, step_row, 0),
                    )
                    out[k, j] = mask * (stay * x + u * xu + v * xv)
        return 0

    lax.fori_loop(0, bins, level, 0)
    for field, ref in enumerate((fo_ref, go_ref)):
        down_ref[field] = ref[:FH]
        up_ref[field] = ref[bins - FH :]


def source_kernel(plan, packs, freq_ref, dir_ref, coupling_ref, f_ref, g_ref, above_ref, below_ref, mask_ref, fo_ref, go_ref, *message_refs):
    bins, nd = plan.bins, plan.nd
    p, q = freq_ref[0], freq_ref[1]
    e, h = dir_ref[0], dir_ref[1]

    def wrap(j):
        return jnp.where(j >= nd, j - nd, jnp.where(j < 0, j + nd, j))

    def level(upper, lower, k, _):
        strength = source_step * coupling_ref[k]

        def direction(j, _):
            f0, g0 = f_ref[k, j], g_ref[k, j]
            up_one, up_two = wrap(j + e), wrap(j - e)
            low_one, low_two = wrap(j - h), wrap(j + h)
            fp1, gp1 = upper(k, up_one)
            fp2, gp2 = upper(k, up_two)
            fm1, gm1 = lower(k, low_one)
            fm2, gm2 = lower(k, low_two)
            linear = weight_plus * (fp1 + fp2) + weight_minus * (fm1 + fm2)
            linear_t = weight_plus * (gp1 + gp2) + weight_minus * (gm1 + gm2)
            cross = weight_cross * (fp1 * fm1 + fp2 * fm2)
            cross_t = weight_cross * ((gp1 * fm1 + fp1 * gm1) + (gp2 * fm2 + fp2 * gm2))
            f0l = f0 * linear
            both = f0l - cross
            rate = f0 * both
            change = g0 * (f0l + both) + f0 * (f0 * linear_t - cross_t)
            fo_ref[k, j] = f0 - strength * rate
            go_ref[k, j] = g0 - strength * change
            return 0

        lax.fori_loop(0, nd, direction, 0, unroll=4)
        return 0

    def own_upper(k, j):
        return f_ref[k + p, j], g_ref[k + p, j]

    def own_lower(k, j):
        return f_ref[k - q, j], g_ref[k - q, j]

    def sent_upper(k, j):
        return above_ref[0, k + p - bins, j], above_ref[1, k + p - bins, j]

    def sent_lower(k, j):
        return below_ref[0, k - q + FH, j], below_ref[1, k - q + FH, j]

    lax.fori_loop(q, bins - p, functools.partial(level, own_upper, own_lower), 0)
    lax.fori_loop(0, q, functools.partial(level, own_upper, sent_lower), 0)
    lax.fori_loop(bins - p, bins, functools.partial(level, sent_upper, own_lower), 0)
    if packs:
        pack(plan, fo_ref, go_ref, mask_ref[...].astype(f32), *message_refs)


def params():
    return pltpu.CompilerParams(vmem_limit_bytes=16 * 1024 * 1024)


def body(background, tangent, sea_mask, coupling, freq_offsets, dir_offsets):
    bins, nd = background.shape[:2]
    rows, lanes = background.shape[-2:]
    plan = Plan(bins, nd, rows, lanes)
    f = background.reshape(bins, nd, rows, lanes)
    g = tangent.reshape(bins, nd, rows, lanes)
    mask = sea_mask.reshape(rows, lanes)
    bands, tiles = lax.axis_size("band"), lax.axis_size("tile")
    speed = jnp.asarray((0.7 * 1.1 ** -np.arange(bands * bins, dtype=np.float64)).astype(np.float32))
    table = jnp.asarray(plan.lane_table())
    field = jax.ShapeDtypeStruct(f.shape, f32)
    row_out = jax.ShapeDtypeStruct(plan.row_shape(), f32)
    col_out = jax.ShapeDtypeStruct(plan.col_shape(), f32)
    band_out = jax.ShapeDtypeStruct((2, FH, nd, rows, lanes), f32)

    def latitude(device):
        return (device + TY // 2) % TY

    northward = [(i, (i + 1) % tiles) for i in range(tiles) if latitude(i) < TY - 1]
    southward = [((i + 1) % tiles, i) for i in range(tiles) if latitude(i) < TY - 1]
    eastward = [(i, (i + TY) % tiles) for i in range(tiles)]
    westward = [((i + TY) % tiles, i) for i in range(tiles)]

    def spatial(north, south, cols):
        from_south = lax.ppermute(north, "tile", northward)
        from_north = lax.ppermute(south, "tile", southward)
        if tiles == 2 * TY:
            beside = lax.ppermute(cols, "tile", eastward)
        else:
            beside = jnp.concatenate(
                [lax.ppermute(cols[:1], "tile", eastward), lax.ppermute(cols[1:], "tile", westward)]
            )
        below = lax.ppermute(beside[:, : 2 * plan.groups, rows - 1 :, :], "tile", northward)
        above = lax.ppermute(beside[:, : 2 * plan.groups, :1, :], "tile", southward)
        return from_south, from_north, beside, below, above

    messages = pl.pallas_call(
        functools.partial(pack_kernel, plan),
        out_shape=(row_out, row_out, col_out),
        in_specs=[VM] * 3,
        out_specs=(VM,) * 3,
        compiler_params=params(),
        name="pack",
    )(f, g, mask)
    for step in range(STEPS):
        from_south, from_north, beside, below, above = spatial(*messages)
        f, g, top, bottom = pl.pallas_call(
            functools.partial(propagate_kernel, plan),
            out_shape=(field, field, band_out, band_out),
            in_specs=[SM] + [VM] * 9,
            out_specs=(VM,) * 4,
            scratch_shapes=[pltpu.VMEM(plan.row_shape(), f32), pltpu.VMEM((2, 2 * plan.groups) + plan.tile, f32)],
            compiler_params=params(),
            name="propagate",
        )(speed, f, g, mask, from_south, from_north, beside, below, above, table)
        from_above = lax.ppermute(bottom, "band", [(i + 1, i) for i in range(bands - 1)])
        from_below = lax.ppermute(top, "band", [(i, i + 1) for i in range(bands - 1)])
        packs = step < STEPS - 1
        f, g, *messages = pl.pallas_call(
            functools.partial(source_kernel, plan, packs),
            out_shape=(field, field) + ((row_out, row_out, col_out) if packs else ()),
            in_specs=[SM] * 3 + [VM] * 5,
            out_specs=(VM,) * (5 if packs else 2),
            compiler_params=params(),
            name="source",
        )(freq_offsets, dir_offsets, coupling, f, g, from_above, from_below, mask)
    return f.reshape(background.shape), g.reshape(tangent.shape)


def solution(mesh):
    in_specs = (
        P("band", None, "tile", None, None),
        P("band", None, "tile", None, None),
        P("tile", None, None),
        P("band"),
        P(),
        P(),
    )
    out_specs = (P("band", None, "tile", None, None), P("band", None, "tile", None, None))
    return jax.shard_map(body, mesh=mesh, in_specs=in_specs, out_specs=out_specs, check_vma=False)
```

```python
import functools
import math

import jax
import jax.numpy as jnp
import numpy as np
from jax import lax
from jax.experimental import pallas as pl
from jax.experimental.pallas import tpu as pltpu
from jax.sharding import PartitionSpec as P

TY = 4
FH = 3
STEPS = 2

weight_plus = 1.0 / 1.25**4
weight_minus = 1.0 / 0.75**4
weight_cross = 1.0 / (1.0 - 0.25**2) ** 4
source_step = 0.5

VM = pl.BlockSpec(memory_space=pltpu.VMEM)
SM = pl.BlockSpec(memory_space=pltpu.SMEM)
ANY = pl.BlockSpec(memory_space=pl.ANY)
f32 = jnp.float32
STAGES = 3


def rotate(x, shift, axis):
    shift = shift % x.shape[axis]
    return x if shift == 0 else pltpu.roll(x, shift, axis)


class Plan:
    def __init__(self, bins, nd, rows, lanes):
        self.bins, self.nd, self.rows, self.lanes = bins, nd, rows, lanes
        self.half, self.quad = nd // 2, nd // 4
        self.group = lanes // nd
        self.groups = -(-bins // self.group)
        self.angles = (np.arange(self.quad) + 0.5) * (2.0 * math.pi / nd)
        self.cosines = [math.cos(a) for a in self.angles]
        self.sines = [math.sin(a) for a in self.angles]
        self.tile = (rows, lanes)
        self.levels = bins + 2 * FH
        self.last = bins * self.quad

    def pair(self, sign, i):
        return (i, self.half - 1 - i) if sign == 0 else (self.nd - 1 - i, self.half + i)

    def lane_table(self):
        table = np.zeros(self.tile, np.float32)
        for lane in range(self.group * self.nd):
            i = (lane % self.nd) // 2 % self.quad
            table[0, lane] = self.cosines[i]
            table[1, lane] = self.sines[i]
        return table


def iotas(plan):
    sub = lax.broadcasted_iota(jnp.int32, plan.tile, 0)
    lane = lax.broadcasted_iota(jnp.int32, plan.tile, 1)
    return sub, lane


def pack_rows(plan, sign, k, f_ref, g_ref, out_ref):
    sub, _ = iotas(plan)
    start = plan.rows - 2 if sign == 0 else 0
    for i in range(plan.quad):
        tiles = [ref[k, j] for j in plan.pair(sign, i) for ref in (f_ref, g_ref)]
        edge = rotate(tiles[3], 6 - start, 0)
        for n in (2, 1, 0):
            edge = jnp.where(sub < 2 * n + 2, rotate(tiles[n], 2 * n - start, 0), edge)
        out_ref[k * plan.quad + i] = edge


def load_kernel(plan, f_hbm, g_hbm, mask_ref, f_ref, g_ref, north_ref, sems):
    mask = mask_ref[...].astype(f32)
    pairs = ((f_hbm, f_ref), (g_hbm, g_ref))
    copies = [
        [pltpu.make_async_copy(src.at[k], dst.at[k], sems.at[n, k]) for n, (src, dst) in enumerate(pairs)]
        for k in range(plan.bins)
    ]
    for level in copies:
        for copy in level:
            copy.start()
    north_ref[plan.last] = mask
    for k in range(plan.bins):
        for copy in copies[k]:
            copy.wait()

        def clear(j, _):
            f_ref[k, j] = f_ref[k, j] * mask
            g_ref[k, j] = g_ref[k, j] * mask
            return 0

        lax.fori_loop(0, plan.nd, clear, 0, unroll=12)
        pack_rows(plan, 0, k, f_ref, g_ref, north_ref)


def pack_kernel(plan, f_ref, g_ref, mask_ref, south_ref, col_ref, corner_n_ref, corner_s_ref):
    mask = mask_ref[...].astype(f32)
    _, lane = iotas(plan)
    pair_lane = lane // 2
    rows, lanes = plan.tile
    south_ref[plan.last] = mask
    for side in range(2):
        col_ref[side, 2 * plan.groups] = mask

    def part(at, _):
        packed = [[jnp.zeros(plan.tile, f32) for _ in range(2)] for _ in range(2)]
        for n in range(plan.group):
            k = jnp.minimum(at * plan.group + n, plan.bins - 1)
            pack_rows(plan, 1, k, f_ref, g_ref, south_ref)
            for sign in range(2):
                for i in range(plan.quad):
                    slot = n * plan.nd // 2 + sign * plan.quad + i
                    for side, j in enumerate(plan.pair(sign, i)):
                        shift = 2 * slot - (lanes - 2 if side == 0 else 0)
                        for field, ref in enumerate((f_ref, g_ref)):
                            packed[side][field] = jnp.where(
                                pair_lane == slot, rotate(ref[k, j], shift, 1), packed[side][field]
                            )
        for side in range(2):
            for field in range(2):
                where = field * plan.groups + at
                value = packed[side][field]
                col_ref[side, where] = value
                corner_n_ref[side, pl.ds(where, 1), :] = value[rows - 1 : rows]
                corner_s_ref[side, pl.ds(where, 1), :] = value[0:1]
        return 0

    lax.fori_loop(0, plan.groups, part, 0)


def side_columns(plan, sign, base, speed_ref, row_mask, col_ref, corner_ref, table_ref, col_both):
    sub, lane = iotas(plan)
    rows, lanes = plan.tile
    in_group = lane // plan.nd
    odd = lane % 2 == 1
    edge_row = 0 if sign == 0 else rows - 1
    for side in range(2):
        edge_lane = lanes - 1 if side == 0 else 0
        near = jnp.broadcast_to(col_ref[side, 2 * plan.groups, :, edge_lane : edge_lane + 1], plan.tile)
        own_lane = lanes - 1 - edge_lane
        corner_mask = jnp.broadcast_to(row_mask[0:1, own_lane : own_lane + 1], plan.tile)
        corner_mask = jnp.where(sub == edge_row, corner_mask, 0.0)
        for part in range(plan.groups):
            speeds = jnp.zeros(plan.tile, f32)
            for n in range(plan.group):
                k = part * plan.group + n
                if k < plan.bins:
                    speeds = jnp.where(in_group == n, speed_ref[base + k], speeds)
            ua = speeds * jnp.broadcast_to(table_ref[0:1, :], plan.tile)
            va = speeds * jnp.broadcast_to(table_ref[1:2, :], plan.tile)
            stay = 1.0 - ua - va
            for field in range(2):
                at = field * plan.groups + part
                here = col_ref[side, at]
                corner = jnp.broadcast_to(corner_ref[side, at : at + 1, :], plan.tile)
                across = rotate(here, 1 if side == 0 else -1, 1)
                along = jnp.where(sub == edge_row, corner, rotate(here, 1 if sign == 0 else -1, 0))
                after = near * (stay * here + ua * across + va * along)
                after = after + va * (corner_mask * corner)
                if side == 0:
                    col_both[side, at] = jnp.where(odd, here, rotate(after, -1, 1))
                else:
                    col_both[side, at] = jnp.where(odd, rotate(after, 1, 1), here)


def propagate_kernel(
    plan, sign, speed_ref, f_ref, g_ref, mask_ref, row_ref, col_ref, corner_ref, table_ref, *refs
):
    ext_ref, up_ref, down_ref, row_next, col_both, *scratch = refs[1:] if sign == 1 else refs
    columns_ref, first_ref, after_ref, second_ref = (scratch[n * STAGES : (n + 1) * STAGES] for n in range(4))
    sub, lane = iotas(plan)
    rows, lanes = plan.tile
    bins, quad, nd = plan.bins, plan.quad, plan.nd
    mask = mask_ref[...].astype(f32)
    base = lax.axis_index("band") * bins
    edge_row = 0 if sign == 0 else rows - 1
    step_row = 1 if sign == 0 else -1
    halo_row = rows - 1 - edge_row
    row_mask = jnp.broadcast_to(row_ref[plan.last, halo_row : halo_row + 1, :], plan.tile)
    first_half = sub < rows // 2
    outer = (first_half & (lane == 0)) | (~first_half & (lane == lanes - 1))
    side_columns(plan, sign, base, speed_ref, row_mask, col_ref, corner_ref, table_ref, col_both)
    fields = (f_ref, g_ref)

    def tiles():
        for i in range(quad):
            for side, j in enumerate(plan.pair(sign, i)):
                for field in range(2):
                    yield i, side, j, field, 4 * i + 2 * side + field

    def weights(k, i):
        speed = speed_ref[base + k]
        u, v = speed * plan.cosines[i], speed * plan.sines[i]
        return 1.0 - u - v, u, v

    def near_lane(side):
        return 0 if side == 0 else lanes - 1

    def gather(k, slot):
        place = lax.rem(k, plan.group)
        back = lax.rem(lanes - place * nd, lanes)
        columns = [
            [pltpu.roll(col_both[side, field * plan.groups + lax.div(k, plan.group)], back, 1) for field in range(2)]
            for side in range(2)
        ]
        for i, side, j, field, at in tiles():
            lane_at = 2 * (sign * quad + i)
            column = rotate(columns[side][field], -(lane_at + 1) if side == 0 else lanes - 1 - lane_at, 1)
            columns_ref[slot][at] = column
            moved = rotate(fields[field][k, j], 1 if side == 0 else -1, 1)
            first_ref[slot][at] = jnp.where(lane == near_lane(side), column, moved)
        for i in range(quad):
            stay, u, v = weights(k, i)
            halo = row_ref[k * quad + i]
            across = jnp.where(first_half, rotate(halo, 1, 1), rotate(halo, -1, 1))
            across = jnp.where(outer, 0.0, across)
            row_next[k * quad + i] = row_mask * (stay * halo + u * across + v * rotate(halo, step_row, 0))

    def beside(x, halo_ref, k, i, side, field):
        inner = 4 * side + 2 * field + 1 - sign
        halo = jnp.broadcast_to(halo_ref[k * quad + i, inner : inner + 1, :], plan.tile)
        return jnp.where(sub == edge_row, halo, rotate(x, step_row, 0))

    def first(k, slot):
        for i, side, j, field, at in tiles():
            stay, u, v = weights(k, i)
            x = fields[field][k, j]
            x = mask * (stay * x + u * first_ref[slot][at] + v * beside(x, row_ref, k, i, side, field))
            after_ref[slot][at] = x
            far = lanes - 1 - near_lane(side)
            second_ref[slot][at] = rotate(
                jnp.where(lane == far, columns_ref[slot][at], x), 1 if side == 0 else -1, 1
            )

    def second(k, slot):
        for i, side, j, field, at in tiles():
            stay, u, v = weights(k, i)
            x = after_ref[slot][at]
            x = mask * (stay * x + u * second_ref[slot][at] + v * beside(x, row_next, k, i, side, field))
            ext_ref[field, (FH + k) * nd + j] = x

    def clamp(k):
        return jnp.clip(k, 0, bins - 1)

    def turn(t, _):
        for n in range(STAGES):
            at = t * STAGES + n
            second(clamp(at - 2), (n - 2) % STAGES)
            first(clamp(at - 1), (n - 1) % STAGES)
            gather(clamp(at), n)
        return 0

    lax.fori_loop(0, -(-(bins + 2) // STAGES), turn, 0)
    start = sign * plan.half
    for field in range(2):
        for n in range(FH):
            down_ref[field, n] = ext_ref[field, pl.ds((FH + n) * nd + start, plan.half)]
            up_ref[field, n] = ext_ref[field, pl.ds((bins + n) * nd + start, plan.half)]


def source_levels(plan, levels, freq_ref, dir_ref, coupling_ref, ext_ref, fo_ref, go_ref, first, last):
    bins, nd = plan.bins, plan.nd
    p, q = freq_ref[0], freq_ref[1]
    e, h = dir_ref[0], dir_ref[1]
    span = (bins - 1) * nd + 1

    def wrap(j):
        return jnp.where(j >= nd, j - nd, jnp.where(j < 0, j + nd, j))

    def direction(j, _):
        def at(field, level, where):
            return ext_ref.at[field, pl.ds(level * nd + where, span)]

        own = [at(field, FH, j) for field in range(2)]
        up_one = [at(field, FH + p, wrap(j + e)) for field in range(2)]
        up_two = [at(field, FH + p, wrap(j - e)) for field in range(2)]
        low_one = [at(field, FH - q, wrap(j - h)) for field in range(2)]
        low_two = [at(field, FH - q, wrap(j + h)) for field in range(2)]
        out_f, out_g = (ref.at[pl.ds(j, span)] for ref in (fo_ref, go_ref))
        for k in levels:
            n = k * nd
            strength = source_step * coupling_ref[k]
            f0, g0 = own[0][n], own[1][n]
            fp1, gp1 = up_one[0][n], up_one[1][n]
            fp2, gp2 = up_two[0][n], up_two[1][n]
            fm1, gm1 = low_one[0][n], low_one[1][n]
            fm2, gm2 = low_two[0][n], low_two[1][n]
            linear = weight_plus * (fp1 + fp2) + weight_minus * (fm1 + fm2)
            linear_t = weight_plus * (gp1 + gp2) + weight_minus * (gm1 + gm2)
            cross = weight_cross * (fp1 * fm1 + fp2 * fm2)
            cross_t = weight_cross * ((gp1 * fm1 + fp1 * gm1) + (gp2 * fm2 + fp2 * gm2))
            f0l = f0 * linear
            both = f0l - cross
            rate = f0 * both
            change = g0 * (f0l + both) + f0 * (f0 * linear_t - cross_t)
            out_f[n] = f0 - strength * rate
            out_g[n] = g0 - strength * change
        return 0

    lax.fori_loop(first, last, direction, 0)


def fill_bands(plan, ext_ref, sent):
    for sign in range(2):
        above_ref, below_ref = sent[2 * sign : 2 * sign + 2]
        start = sign * plan.half
        for field in range(2):
            for n in range(FH):
                ext_ref[field, pl.ds(n * plan.nd + start, plan.half)] = below_ref[field, n]
                top = (FH + plan.bins + n) * plan.nd + start
                ext_ref[field, pl.ds(top, plan.half)] = above_ref[field, n]


def source_kernel(plan, freq_ref, dir_ref, coupling_ref, ext_in, a, b, c, d, mask_ref, ext_ref, f_ref, g_ref, north_ref):
    fill_bands(plan, ext_ref, (a, b, c, d))
    flat = [ref.reshape((plan.bins * plan.nd,) + plan.tile) for ref in (f_ref, g_ref)]
    source_levels(plan, range(plan.bins), freq_ref, dir_ref, coupling_ref, ext_ref, *flat, 0, plan.nd)
    north_ref[plan.last] = mask_ref[...].astype(f32)

    def rows(k, _):
        pack_rows(plan, 0, k, f_ref, g_ref, north_ref)
        return 0

    lax.fori_loop(0, plan.bins, rows, 0)


def last_kernel(plan, chunks, freq_ref, dir_ref, coupling_ref, ext_in, a, b, c, d, ext_ref, f_hbm, g_hbm, f_ref, g_ref, sems):
    fill_bands(plan, ext_ref, (a, b, c, d))
    flat = [ref.reshape((plan.bins * plan.nd,) + plan.tile) for ref in (f_ref, g_ref)]
    each = plan.nd // chunks
    copies = []
    for n in range(chunks):
        source_levels(
            plan, range(plan.bins), freq_ref, dir_ref, coupling_ref, ext_ref, *flat, n * each, (n + 1) * each
        )
        part = pl.ds(n * each, each)
        for field, (src, dst) in enumerate(((f_ref, f_hbm), (g_ref, g_hbm))):
            copies.append(pltpu.make_async_copy(src.at[:, part], dst.at[:, part], sems.at[field, n]))
            copies[-1].start()
    for copy in copies:
        copy.wait()


def params():
    return pltpu.CompilerParams(vmem_limit_bytes=16 * 1024 * 1024)


def body(background, tangent, sea_mask, coupling, freq_offsets, dir_offsets):
    bins, nd = background.shape[:2]
    rows, lanes = background.shape[-2:]
    plan = Plan(bins, nd, rows, lanes)
    f = background.reshape(bins, nd, rows, lanes)
    g = tangent.reshape(bins, nd, rows, lanes)
    mask = sea_mask.reshape(rows, lanes)
    bands, tiles = lax.axis_size("band"), lax.axis_size("tile")
    speed = jnp.asarray((0.7 * 1.1 ** -np.arange(bands * bins, dtype=np.float64)).astype(np.float32))
    table = jnp.asarray(plan.lane_table())

    def array(*shape):
        return jax.ShapeDtypeStruct(shape + plan.tile, f32)

    field = array(bins, nd)
    ext_out = array(2, plan.levels * nd)
    row_out = array(plan.last + 1)
    col_out = array(2, 2 * plan.groups + 1)
    corner_out = jax.ShapeDtypeStruct((2, -(-2 * plan.groups // 8) * 8, lanes), f32)
    band_out = array(2, FH, plan.half)

    def moves(north, east):
        pairs = []
        for i in range(tiles):
            g = (i + TY // 2) % tiles
            row = g % TY + north
            if 0 <= row < TY:
                g = (g // TY * TY + row + east * TY) % tiles
                pairs.append((i, (g - TY // 2) % tiles))
        return pairs

    def tile_move(value, north, east):
        return lax.ppermute(value, "tile", moves(north, east))

    def sideways(value, north):
        if tiles == 2 * TY:
            return tile_move(value, north, 1)
        return jnp.concatenate([tile_move(value[:1], north, 1), tile_move(value[1:], north, -1)])

    f, g, north = pl.pallas_call(
        functools.partial(load_kernel, plan),
        out_shape=(field, field, row_out),
        in_specs=[ANY, ANY, VM],
        out_specs=(VM,) * 3,
        scratch_shapes=[pltpu.SemaphoreType.DMA((2, bins))],
        compiler_params=params(),
        name="load",
    )(f, g, mask)
    for step in range(STEPS):
        from_south = tile_move(north, 1, 0)
        south, cols, corner_n, corner_s = pl.pallas_call(
            functools.partial(pack_kernel, plan),
            out_shape=(row_out, col_out, corner_out, corner_out),
            in_specs=[VM] * 3,
            out_specs=(VM,) * 4,
            compiler_params=params(),
            name="pack",
        )(f, g, mask)
        beside = sideways(cols, 0)
        corners = (sideways(corner_n, 1), sideways(corner_s, -1))
        from_north = tile_move(south, -1, 0)
        ext = None
        sent = []
        for sign, message in enumerate((from_south, from_north)):
            args = (speed, f, g, mask, message, beside, corners[sign], table) + ((ext,) if sign else ())
            ext, top, bottom = pl.pallas_call(
                functools.partial(propagate_kernel, plan, sign),
                out_shape=(ext_out, band_out, band_out),
                in_specs=[SM] + [VM] * (len(args) - 1),
                out_specs=(VM,) * 3,
                scratch_shapes=[
                    pltpu.VMEM((plan.last,) + plan.tile, f32),
                    pltpu.VMEM((2, 2 * plan.groups) + plan.tile, f32),
                ]
                + [pltpu.VMEM((2 * plan.half,) + plan.tile, f32)] * (4 * STAGES),
                input_output_aliases={8: 0} if sign else {},
                compiler_params=params(),
                name=("north", "south")[sign],
            )(*args)
            sent.append(lax.ppermute(bottom, "band", [(i + 1, i) for i in range(bands - 1)]))
            sent.append(lax.ppermute(top, "band", [(i, i + 1) for i in range(bands - 1)]))
        if step < STEPS - 1:
            _, f, g, north = pl.pallas_call(
                functools.partial(source_kernel, plan),
                out_shape=(ext_out, field, field, row_out),
                in_specs=[SM] * 3 + [VM] * 6,
                out_specs=(VM,) * 4,
                input_output_aliases={3: 0},
                compiler_params=params(),
                name="source",
            )(freq_offsets, dir_offsets, coupling, ext, *sent, mask)
        else:
            chunks = 6
            _, f, g = pl.pallas_call(
                functools.partial(last_kernel, plan, chunks),
                out_shape=(ext_out, field, field),
                in_specs=[SM] * 3 + [VM] * 5,
                out_specs=(VM, ANY, ANY),
                scratch_shapes=[pltpu.VMEM(field.shape, f32)] * 2 + [pltpu.SemaphoreType.DMA((2, chunks))],
                input_output_aliases={3: 0},
                compiler_params=params(),
                name="last",
            )(freq_offsets, dir_offsets, coupling, ext, *sent)
    return f.reshape(background.shape), g.reshape(tangent.shape)


def solution(mesh):
    in_specs = (
        P("band", None, "tile", None, None),
        P("band", None, "tile", None, None),
        P("tile", None, None),
        P("band"),
        P(),
        P(),
    )
    out_specs = (P("band", None, "tile", None, None), P("band", None, "tile", None, None))
    return jax.shard_map(body, mesh=mesh, in_specs=in_specs, out_specs=out_specs, check_vma=False)
```

```python
import functools
import math

import jax
import jax.numpy as jnp
import numpy as np
from jax import lax
from jax.experimental import pallas as pl
from jax.experimental.pallas import tpu as pltpu
from jax.sharding import PartitionSpec as P

TY = 4
FH = 3
STEPS = 2

weight_plus = 1.0 / 1.25**4
weight_minus = 1.0 / 0.75**4
weight_cross = 1.0 / (1.0 - 0.25**2) ** 4
source_step = 0.5

VM = pl.BlockSpec(memory_space=pltpu.VMEM)
SM = pl.BlockSpec(memory_space=pltpu.SMEM)
HBM = pl.BlockSpec(memory_space=pltpu.HBM)
f32 = jnp.float32
STAGES = 2


def rotate(x, shift, axis):
    shift = shift % x.shape[axis]
    return x if shift == 0 else pltpu.roll(x, shift, axis)


class Plan:
    def __init__(self, bins, nd, rows, lanes):
        self.bins, self.nd, self.rows, self.lanes = bins, nd, rows, lanes
        self.half, self.quad = nd // 2, nd // 4
        self.group = lanes // nd
        self.groups = bins // self.group
        assert self.group == FH and bins == FH * self.groups and nd == 4 * self.quad and bins >= 2 * FH
        angles = (np.arange(self.quad) + 0.5) * (2.0 * math.pi / nd)
        self.cosines, self.sines = np.cos(angles), np.sin(angles)
        self.tile = (rows, lanes)
        self.levels = bins + 2 * FH
        self.last = bins * self.quad
        self.weight_tiles = -(-3 * self.quad // rows)
        self.sent_rows = FH * self.quad
        self.sent = 2 * self.sent_rows + 5

    def pair(self, sign, i):
        return (i, self.half - 1 - i) if sign == 0 else (self.nd - 1 - i, self.half + i)

    def tiles(self):
        for sign in range(2):
            for i in range(self.quad):
                for side, j in enumerate(self.pair(sign, i)):
                    for field in range(2):
                        yield sign, i, side, j, field, 4 * (sign * self.quad + i) + 2 * side + field

    def table(self):
        n, rows, lanes = self.weight_tiles, self.rows, self.lanes
        table = np.zeros((2 * n + 1, rows, lanes), np.float32)
        for i in range(self.quad):
            for c, (slope, rest) in enumerate(
                ((-self.cosines[i] - self.sines[i], 1.0), (self.cosines[i], 0.0), (self.sines[i], 0.0))
            ):
                t, row = divmod(3 * i + c, rows)
                table[t, row], table[n + t, row] = slope, rest
        for lane in range(self.group * self.nd):
            i = (lane % self.nd) // 2 % self.quad
            table[2 * n, 0, lane], table[2 * n, 1, lane] = self.cosines[i], self.sines[i]
        return table


def iotas(plan):
    sub = lax.broadcasted_iota(jnp.int32, plan.tile, 0)
    lane = lax.broadcasted_iota(jnp.int32, plan.tile, 1)
    return sub, lane


def row_parity():
    return lax.rem(lax.rem(lax.axis_index("tile") + TY // 2, TY), 2)


def band_parity():
    return lax.rem(lax.axis_index("band"), 2)


def spread(row, plan):
    return jnp.broadcast_to(row, plan.tile)


def pack_rows(plan, k, f_ref, g_ref, out_ref):
    sub, _ = iotas(plan)
    for sign in range(2):
        start = plan.rows - 2 if sign == 0 else 0
        for i in range(plan.quad):
            tiles = [ref[k, j] for j in plan.pair(sign, i) for ref in (f_ref, g_ref)]
            edge = rotate(tiles[3], 6 - start, 0)
            for n in (2, 1, 0):
                edge = jnp.where(sub < 2 * n + 2, rotate(tiles[n], 2 * n - start, 0), edge)
            out_ref[sign, k * plan.quad + i] = edge


def send_out(plan, f_ref, g_ref, rows_ref, row_refs, raw_refs):
    parity, band = row_parity(), band_parity()
    for n in range(2):
        towards = parity if n == 0 else 1 - parity
        row_refs[n][...] = rows_ref[towards]
        start = (band if n == 1 else 1 - band) * (plan.bins - FH)
        for field, ref in enumerate((f_ref, g_ref)):
            raw_refs[n][field] = ref[pl.ds(start, FH)]


def load_kernel(plan, speed_ref, f_hbm, g_hbm, mask_ref, table_ref, f_ref, g_ref, even_ref, odd_ref, raw_even, raw_odd, weight_ref, rows_ref, sems):
    mask = mask_ref[...].astype(f32)
    pairs = ((f_hbm, f_ref), (g_hbm, g_ref))
    copies = [
        [pltpu.make_async_copy(src.at[k], dst.at[k], sems.at[n, k]) for n, (src, dst) in enumerate(pairs)]
        for k in range(plan.bins)
    ]
    for level in copies:
        for copy in level:
            copy.start()
    base = lax.axis_index("band") * plan.bins
    for level in range(plan.levels):
        speed = speed_ref[base + level]
        for t in range(plan.weight_tiles):
            weight_ref[level, t] = table_ref[plan.weight_tiles + t] + speed * table_ref[t]
    for sign in range(2):
        rows_ref[sign, plan.last] = mask
    for k in range(plan.bins):
        for copy in copies[k]:
            copy.wait()

        def clear(j, _):
            f_ref[k, j] = f_ref[k, j] * mask
            g_ref[k, j] = g_ref[k, j] * mask
            return 0

        lax.fori_loop(0, plan.nd, clear, 0, unroll=12)
    lax.fori_loop(0, plan.bins, lambda k, _: pack_rows(plan, k, f_ref, g_ref, rows_ref) or 0, 0)
    send_out(plan, f_ref, g_ref, rows_ref, (even_ref, odd_ref), (raw_even, raw_odd))


def pack_kernel(plan, f_ref, g_ref, mask_ref, col_ref, even_ref, odd_ref):
    mask = mask_ref[...].astype(f32)
    _, lane = iotas(plan)
    pair_lane = lane // 2
    rows, lanes = plan.tile
    upward = row_parity() == 0
    for side in range(2):
        col_ref[side, 2 * plan.groups] = mask

    def part(at, _):
        packed = [[jnp.zeros(plan.tile, f32) for _ in range(2)] for _ in range(2)]
        for n in range(plan.group):
            for sign, i, side, j, field, _ in plan.tiles():
                slot = n * plan.half + sign * plan.quad + i
                shift = 2 * slot - (lanes - 2 if side == 0 else 0)
                value = rotate((f_ref, g_ref)[field][at * plan.group + n, j], shift, 1)
                packed[side][field] = jnp.where(pair_lane == slot, value, packed[side][field])
        for side in range(2):
            for field in range(2):
                where = field * plan.groups + at
                value = packed[side][field]
                col_ref[side, where] = value
                top, bottom = value[rows - 1 : rows], value[0:1]
                even_ref[side, pl.ds(where, 1), :] = jnp.where(upward, top, bottom)
                odd_ref[side, pl.ds(where, 1), :] = jnp.where(upward, bottom, top)
        return 0

    lax.fori_loop(0, plan.groups, part, 0)


def forward_kernel(plan, even_ref, odd_ref, col_ref, corner_even, corner_odd, rows_ref, corner_ref, fwd_even, fwd_odd):
    parity, band = row_parity(), band_parity()
    rows_ref[1 - parity] = even_ref[...]
    rows_ref[parity] = odd_ref[...]
    corner_ref[1 - parity] = corner_even[...]
    corner_ref[parity] = corner_odd[...]
    for n, out in enumerate((fwd_even, fwd_odd)):
        top = band if n == 1 else 1 - band
        part = top * (plan.groups - 1)
        start = top * (plan.bins - FH) * plan.quad
        for sign in range(2):
            out[sign * plan.sent_rows : (sign + 1) * plan.sent_rows] = rows_ref[sign, pl.ds(start, plan.sent_rows)]
            for side in range(2):
                for field in range(2):
                    row = 4 * sign + 2 * side + field
                    at = field * plan.groups + part
                    out[plan.sent - 1, row : row + 1, :] = corner_ref[sign, side, pl.ds(at, 1), :]
                    out[2 * plan.sent_rows + 2 * side + field] = col_ref[side, at]


def side_columns(plan, masks, speeds, sides, table_ref, here_at, corner_at, out_at):
    sub, lane = iotas(plan)
    rows, lanes = plan.tile
    in_group = lane // plan.nd
    odd = lane % 2 == 1
    northward = (lane % plan.nd) // 2 < plan.quad
    lane_table = 2 * plan.weight_tiles
    speed = jnp.where(in_group == 0, speeds[0], jnp.where(in_group == 1, speeds[1], speeds[2]))
    ua = speed * spread(table_ref[lane_table, 0:1, :], plan)
    va = speed * spread(table_ref[lane_table, 1:2, :], plan)
    stay = 1.0 - ua - va
    for side in range(2):
        near, corner_masks = sides[side]
        for field in range(2):
            here = here_at(side, field)
            below, above = (spread(corner_at(sign, side, field), plan) for sign in range(2))
            across = rotate(here, 1 if side == 0 else -1, 1)
            along = jnp.where(
                northward,
                jnp.where(sub == 0, below, rotate(here, 1, 0)),
                jnp.where(sub == rows - 1, above, rotate(here, -1, 0)),
            )
            after = near * (stay * here + ua * across + va * along)
            corner = jnp.where(northward, corner_masks[0] * below, corner_masks[1] * above)
            after = after + va * corner
            if side == 0:
                out_at(side, field, jnp.where(odd, here, rotate(after, -1, 1)))
            else:
                out_at(side, field, jnp.where(odd, rotate(after, 1, 1), here))


def side_masks(plan, row_masks, col_ref):
    sub, _ = iotas(plan)
    rows, lanes = plan.tile
    sides = []
    for side in range(2):
        edge = lanes - 1 if side == 0 else 0
        own = lanes - 1 - edge
        near = spread(col_ref[side, 2 * plan.groups, :, edge : edge + 1], plan)
        corners = [
            jnp.where(sub == (0, rows - 1)[sign], spread(row_masks[sign][0:1, own : own + 1], plan), 0.0)
            for sign in range(2)
        ]
        sides.append((near, corners))
    return sides


def sweep(plan, count, mask, row_masks, weight_at, field_at, halo_at, column_at, store, scratch):
    rows_after, *rest = scratch
    columns_ref, first_ref, after_ref, second_ref = (rest[n * STAGES : (n + 1) * STAGES] for n in range(4))
    sub, lane = iotas(plan)
    rows, lanes = plan.tile
    first_half = sub < rows // 2
    outer = (first_half & (lane == 0)) | (~first_half & (lane == lanes - 1))
    edge_row, step_row = (0, rows - 1), (1, -1)
    near_lane, into = (0, lanes - 1), (1, -1)

    def weights(k, i):
        return [spread(weight_at(k, *divmod(3 * i + c, rows)), plan) for c in range(3)]

    def beside(x, halo, sign, side, field):
        inner = 4 * side + 2 * field + 1 - sign
        return jnp.where(sub == edge_row[sign], spread(halo(inner), plan), rotate(x, step_row[sign], 0))

    def gather(k, slot):
        columns = [[column_at(k, side, field) for field in range(2)] for side in range(2)]
        for sign, i, side, j, field, at in plan.tiles():
            lane_at = 2 * (sign * plan.quad + i)
            shift = -(lane_at + 1) if side == 0 else lanes - 1 - lane_at
            column = rotate(columns[side][field], shift, 1)
            columns_ref[slot][at] = column
            moved = rotate(field_at(field, k, j), into[side], 1)
            first_ref[slot][at] = jnp.where(lane == near_lane[side], column, moved)
        for i in range(plan.quad):
            stay, u, v = weights(k, i)
            for sign in range(2):
                halo = halo_at(sign, k, i)[...]
                across = jnp.where(first_half, rotate(halo, 1, 1), rotate(halo, -1, 1))
                across = jnp.where(outer, 0.0, across)
                along = rotate(halo, step_row[sign], 0)
                rows_after[sign, k * plan.quad + i] = row_masks[sign] * (stay * halo + u * across + v * along)

    def first(k, slot):
        for sign, i, side, j, field, at in plan.tiles():
            stay, u, v = weights(k, i)
            x = field_at(field, k, j)
            halo = halo_at(sign, k, i)
            y = beside(x, lambda n: halo[n : n + 1, :], sign, side, field)
            x = mask * (stay * x + u * first_ref[slot][at] + v * y)
            after_ref[slot][at] = x
            far = lanes - 1 - near_lane[side]
            second_ref[slot][at] = rotate(jnp.where(lane == far, columns_ref[slot][at], x), into[side], 1)

    def second(k, slot):
        for sign, i, side, j, field, at in plan.tiles():
            stay, u, v = weights(k, i)
            x = after_ref[slot][at]
            halo = rows_after.at[sign, k * plan.quad + i]
            y = beside(x, lambda n: halo[n : n + 1, :], sign, side, field)
            store(field, k, j, mask * (stay * x + u * second_ref[slot][at] + v * y))

    def clamp(k):
        return jnp.clip(k, 0, count - 1)

    def turn(t, _):
        for n in range(STAGES):
            at = t * STAGES + n
            second(clamp(at - 2), (n - 2) % STAGES)
            first(clamp(at - 1), (n - 1) % STAGES)
            gather(clamp(at), n)
        return 0

    lax.fori_loop(0, -(-(count + 2) // STAGES), turn, 0)


def sweep_scratch(plan, count):
    return [pltpu.VMEM((2, count * plan.quad) + plan.tile, f32)] + [
        pltpu.VMEM((2 * plan.nd,) + plan.tile, f32)
    ] * (4 * STAGES)


def halo_masks(plan, rows_ref):
    rows = plan.rows
    return [spread(rows_ref[0, plan.last, rows - 1 : rows, :], plan), spread(rows_ref[1, plan.last, 0:1, :], plan)]


def turned(plan, tile, place):
    back = lax.rem(plan.lanes - place * plan.nd, plan.lanes)
    return pltpu.roll(tile, back, 1)


def own_kernel(plan, speed_ref, f_ref, g_ref, mask_ref, rows_ref, col_ref, corner_ref, table_ref, weight_ref, ext_ref, both_ref, *scratch):
    base = lax.axis_index("band") * plan.bins + FH
    row_masks = halo_masks(plan, rows_ref)
    sides = side_masks(plan, row_masks, col_ref)
    for part in range(plan.groups):

        def put(side, field, value):
            both_ref[side, field, part] = value

        side_columns(
            plan, row_masks, [speed_ref[base + part * plan.group + n] for n in range(plan.group)], sides, table_ref,
            lambda side, field: col_ref[side, field * plan.groups + part],
            lambda sign, side, field: corner_ref[sign, side, pl.ds(field * plan.groups + part, 1), :],
            put,
        )

    def store(field, k, j, value):
        ext_ref[field, (FH + k) * plan.nd + j] = value

    sweep(
        plan, plan.bins, mask_ref[...].astype(f32), row_masks,
        lambda k, t, row: weight_ref[FH + k, t, row : row + 1, :],
        lambda field, k, j: (f_ref, g_ref)[field][k, j],
        lambda sign, k, i: rows_ref.at[sign, k * plan.quad + i],
        lambda k, side, field: turned(plan, both_ref[side, field, lax.div(k, plan.group)], lax.rem(k, plan.group)),
        store, scratch,
    )


def halo_kernel(
    plan, speed_ref, raw_even, raw_odd, fwd_even, fwd_odd, mask_ref, rows_ref, col_ref, table_ref, weight_ref, ext_in,
    ext_ref, raw_ref, fwd_ref, both_ref, *scratch,
):
    band = band_parity()
    for field in range(2):
        raw_ref[field, pl.ds((1 - band) * FH, FH)] = raw_even[field]
        raw_ref[field, pl.ds(band * FH, FH)] = raw_odd[field]
    fwd_ref[1 - band] = fwd_even[...]
    fwd_ref[band] = fwd_odd[...]
    base = lax.axis_index("band") * plan.bins
    row_masks = halo_masks(plan, rows_ref)
    sides = side_masks(plan, row_masks, col_ref)
    for part in range(2):

        def put(side, field, value):
            both_ref[side, field, part] = value

        def corner(sign, side, field):
            row = 4 * sign + 2 * side + field
            return fwd_ref[part, plan.sent - 1, row : row + 1, :]

        side_columns(
            plan, row_masks, [speed_ref[base + part * (FH + plan.bins) + n] for n in range(plan.group)], sides, table_ref,
            lambda side, field: fwd_ref[part, 2 * plan.sent_rows + 2 * side + field],
            corner,
            put,
        )

    def level(k):
        return jnp.where(k < FH, k, k + plan.bins)

    def store(field, k, j, value):
        ext_ref[field, level(k) * plan.nd + j] = value

    def halo(sign, k, i):
        part = jnp.where(k < FH, 0, 1)
        return fwd_ref.at[part, sign * plan.sent_rows + (k - part * FH) * plan.quad + i]

    def column(k, side, field):
        part = jnp.where(k < FH, 0, 1)
        return turned(plan, both_ref[side, field, part], k - part * FH)

    sweep(
        plan, 2 * FH, mask_ref[...].astype(f32), row_masks,
        lambda k, t, row: weight_ref[level(k), t, row : row + 1, :],
        lambda field, k, j: raw_ref[field, k, j],
        halo, column, store, scratch,
    )


def source_levels(plan, freq_ref, dir_ref, coupling_ref, ext_ref, fo_ref, go_ref, first, last):
    bins, nd = plan.bins, plan.nd
    p, q = freq_ref[0], freq_ref[1]
    e, h = dir_ref[0], dir_ref[1]
    span = (bins - 1) * nd + 1

    def wrap(j):
        return jnp.where(j >= nd, j - nd, jnp.where(j < 0, j + nd, j))

    def direction(j, _):
        def at(field, level, where):
            return ext_ref.at[field, pl.ds(level * nd + where, span)]

        own = [at(field, FH, j) for field in range(2)]
        up_one = [at(field, FH + p, wrap(j + e)) for field in range(2)]
        up_two = [at(field, FH + p, wrap(j - e)) for field in range(2)]
        low_one = [at(field, FH - q, wrap(j - h)) for field in range(2)]
        low_two = [at(field, FH - q, wrap(j + h)) for field in range(2)]
        out_f, out_g = (ref.at[pl.ds(j, span)] for ref in (fo_ref, go_ref))
        for k in range(bins):
            n = k * nd
            strength = source_step * coupling_ref[k]
            f0, g0 = own[0][n], own[1][n]
            fp1, gp1 = up_one[0][n], up_one[1][n]
            fp2, gp2 = up_two[0][n], up_two[1][n]
            fm1, gm1 = low_one[0][n], low_one[1][n]
            fm2, gm2 = low_two[0][n], low_two[1][n]
            linear = weight_plus * (fp1 + fp2) + weight_minus * (fm1 + fm2)
            linear_t = weight_plus * (gp1 + gp2) + weight_minus * (gm1 + gm2)
            cross = weight_cross * (fp1 * fm1 + fp2 * fm2)
            cross_t = weight_cross * ((gp1 * fm1 + fp1 * gm1) + (gp2 * fm2 + fp2 * gm2))
            f0l = f0 * linear
            both = f0l - cross
            rate = f0 * both
            change = g0 * (f0l + both) + f0 * (f0 * linear_t - cross_t)
            out_f[n] = f0 - strength * rate
            out_g[n] = g0 - strength * change
        return 0

    lax.fori_loop(first, last, direction, 0)


def flat(plan, ref):
    return ref.reshape((plan.bins * plan.nd,) + plan.tile)


def source_kernel(plan, freq_ref, dir_ref, coupling_ref, ext_ref, mask_ref, f_ref, g_ref, even_ref, odd_ref, raw_even, raw_odd, rows_ref):
    source_levels(plan, freq_ref, dir_ref, coupling_ref, ext_ref, flat(plan, f_ref), flat(plan, g_ref), 0, plan.nd)
    for sign in range(2):
        rows_ref[sign, plan.last] = mask_ref[...].astype(f32)
    lax.fori_loop(0, plan.bins, lambda k, _: pack_rows(plan, k, f_ref, g_ref, rows_ref) or 0, 0)
    send_out(plan, f_ref, g_ref, rows_ref, (even_ref, odd_ref), (raw_even, raw_odd))


def last_kernel(plan, chunks, freq_ref, dir_ref, coupling_ref, ext_ref, f_hbm, g_hbm, f_ref, g_ref, sems):
    each = plan.nd // chunks
    copies = []
    for n in range(chunks):
        source_levels(
            plan, freq_ref, dir_ref, coupling_ref, ext_ref, flat(plan, f_ref), flat(plan, g_ref), n * each, (n + 1) * each
        )
        part = pl.ds(n * each, each)
        for field, (src, dst) in enumerate(((f_ref, f_hbm), (g_ref, g_hbm))):
            copies.append(pltpu.make_async_copy(src.at[:, part], dst.at[:, part], sems.at[field, n]))
            copies[-1].start()
    for copy in copies:
        copy.wait()


def body(background, tangent, sea_mask, coupling, freq_offsets, dir_offsets):
    bins, nd = background.shape[:2]
    rows, lanes = background.shape[-2:]
    plan = Plan(bins, nd, rows, lanes)
    f = background.reshape(bins, nd, rows, lanes)
    g = tangent.reshape(bins, nd, rows, lanes)
    mask = sea_mask.reshape(rows, lanes)
    bands, tiles = lax.axis_size("band"), lax.axis_size("tile")
    levels = np.arange(-FH, bands * bins + FH, dtype=np.float64)
    speed = jnp.asarray((0.7 * 1.1**-levels).astype(np.float32))
    table = jnp.asarray(plan.table())

    def array(*shape):
        return jax.ShapeDtypeStruct(shape + plan.tile, f32)

    field = array(bins, nd)
    ext_out = array(2, plan.levels * nd)
    row_out = array(plan.last + 1)
    col_out = array(2, 2 * plan.groups + 1)
    corner_out = jax.ShapeDtypeStruct((2, -(-2 * plan.groups // 8) * 8, lanes), f32)
    raw_out = array(2, FH, nd)
    fwd_out = array(plan.sent)
    both = pltpu.VMEM((2, 2, plan.groups) + plan.tile, f32)
    sorted_rows = pltpu.VMEM((2, plan.last + 1) + plan.tile, f32)

    def kernel(name, function, out_shape, in_specs, scratch=(), out_specs=None, aliases={}):
        return pl.pallas_call(
            functools.partial(function, plan),
            out_shape=out_shape,
            in_specs=in_specs,
            out_specs=out_specs or (VM,) * len(out_shape),
            scratch_shapes=list(scratch),
            input_output_aliases=aliases,
            compiler_params=pltpu.CompilerParams(vmem_limit_bytes=20 * 1024 * 1024),
            name=name,
        )

    def tile_pairs(parity, east):
        pairs = []
        for i in range(tiles):
            at = (i + TY // 2) % tiles
            row = at % TY
            if parity is not None:
                row += 1 if row % 2 == parity else -1
            if 0 <= row < TY:
                to = (at // TY * TY + row + east * TY) % tiles
                pairs.append((i, (to - TY // 2) % tiles))
        return pairs

    def tile_swap(value, parity):
        return lax.ppermute(value, "tile", tile_pairs(parity, 0))

    def sideways(value, parity):
        if tiles == 2 * TY:
            return lax.ppermute(value, "tile", tile_pairs(parity, 1))
        return jnp.concatenate(
            [lax.ppermute(value[n : n + 1], "tile", tile_pairs(parity, 1 - 2 * n)) for n in range(2)]
        )

    def band_swap(value, parity):
        pairs = [(i, i + 1 if i % 2 == parity else i - 1) for i in range(bands)]
        return lax.ppermute(value, "band", [(a, b) for a, b in pairs if 0 <= b < bands])

    f, g, even, odd, raw_even, raw_odd, weights = kernel(
        "load",
        load_kernel,
        (field, field, row_out, row_out, raw_out, raw_out, array(plan.levels, plan.weight_tiles)),
        [SM, HBM, HBM, VM, VM],
        [sorted_rows, pltpu.SemaphoreType.DMA((2, bins))],
    )(speed, f, g, mask, table)
    for step in range(STEPS):
        even, odd = tile_swap(even, 0), tile_swap(odd, 1)
        raw_odd, raw_even = band_swap(raw_odd, 1), band_swap(raw_even, 0)
        cols, corner_even, corner_odd = kernel(
            "pack", pack_kernel, (col_out, corner_out, corner_out), [VM] * 3
        )(f, g, mask)
        cols = sideways(cols, None)
        corner_even, corner_odd = sideways(corner_even, 0), sideways(corner_odd, 1)
        sorted_out = (array(2, plan.last + 1), jax.ShapeDtypeStruct((2,) + corner_out.shape, f32), fwd_out, fwd_out)
        halo_rows, corners, fwd_even, fwd_odd = kernel("forward", forward_kernel, sorted_out, [VM] * 5)(
            even, odd, cols, corner_even, corner_odd
        )
        fwd_odd, fwd_even = band_swap(fwd_odd, 1), band_swap(fwd_even, 0)
        (ext,) = kernel(
            "own", own_kernel, (ext_out,), [SM] + [VM] * 8, [both] + sweep_scratch(plan, bins)
        )(speed, f, g, mask, halo_rows, cols, corners, table, weights)
        (ext,) = kernel(
            "halo",
            halo_kernel,
            (ext_out,),
            [SM] + [VM] * 10,
            [pltpu.VMEM((2, 2 * FH, nd) + plan.tile, f32), pltpu.VMEM((2, plan.sent) + plan.tile, f32), both]
            + sweep_scratch(plan, 2 * FH),
            aliases={10: 0},
        )(speed, raw_even, raw_odd, fwd_even, fwd_odd, mask, halo_rows, cols, table, weights, ext)
        if step < STEPS - 1:
            f, g, even, odd, raw_even, raw_odd = kernel(
                "source",
                source_kernel,
                (field, field, row_out, row_out, raw_out, raw_out),
                [SM] * 3 + [VM] * 2,
                [sorted_rows],
            )(freq_offsets, dir_offsets, coupling, ext, mask)
        else:
            chunks = 6
            f, g = kernel(
                "last",
                lambda plan, *refs: last_kernel(plan, chunks, *refs),
                (field, field),
                [SM] * 3 + [VM],
                [pltpu.VMEM(field.shape, f32)] * 2 + [pltpu.SemaphoreType.DMA((2, chunks))],
                out_specs=(HBM, HBM),
            )(freq_offsets, dir_offsets, coupling, ext)
    return f.reshape(background.shape), g.reshape(tangent.shape)


def solution(mesh):
    in_specs = (
        P("band", None, "tile", None, None),
        P("band", None, "tile", None, None),
        P("tile", None, None),
        P("band"),
        P(),
        P(),
    )
    out_specs = (P("band", None, "tile", None, None), P("band", None, "tile", None, None))
    return jax.shard_map(body, mesh=mesh, in_specs=in_specs, out_specs=out_specs, check_vma=False)
```

```python
import functools
import math

import jax
import jax.numpy as jnp
import numpy as np
from jax import lax
from jax.experimental import pallas as pl
from jax.experimental.pallas import tpu as pltpu
from jax.sharding import PartitionSpec as P


TY = 4
FH = 3
STEPS = 2

weight_plus = 1.0 / 1.25**4
weight_minus = 1.0 / 0.75**4
weight_cross = 1.0 / (1.0 - 0.25**2) ** 4
source_step = 0.5

VM = pl.BlockSpec(memory_space=pltpu.VMEM)
SM = pl.BlockSpec(memory_space=pltpu.SMEM)
HBM = pl.BlockSpec(memory_space=pltpu.HBM)
f32 = jnp.float32
STAGES = 2


def rotate(x, shift, axis):
    shift = shift % x.shape[axis]
    return x if shift == 0 else pltpu.roll(x, shift, axis)


class Plan:
    def __init__(self, bins, nd, rows, lanes):
        self.bins, self.nd, self.rows, self.lanes = bins, nd, rows, lanes
        self.half, self.quad = nd // 2, nd // 4
        self.group = lanes // nd
        self.groups = bins // self.group
        assert self.group == FH and bins == FH * self.groups and nd == 4 * self.quad and bins >= 2 * FH
        angles = (np.arange(self.quad) + 0.5) * (2.0 * math.pi / nd)
        self.cosines, self.sines = np.cos(angles), np.sin(angles)
        self.tile = (rows, lanes)
        self.levels = bins + 2 * FH
        self.last = bins * self.quad
        self.weight_tiles = -(-3 * self.quad // rows)
        self.sent_rows = FH * self.quad
        self.sent = 2 * self.sent_rows + 5

    def pair(self, sign, i):
        return (i, self.half - 1 - i) if sign == 0 else (self.nd - 1 - i, self.half + i)

    def tiles(self):
        for sign in range(2):
            for i in range(self.quad):
                for side, j in enumerate(self.pair(sign, i)):
                    for field in range(2):
                        yield sign, i, side, j, field, 4 * (sign * self.quad + i) + 2 * side + field


def iotas(plan):
    sub = lax.broadcasted_iota(jnp.int32, plan.tile, 0)
    lane = lax.broadcasted_iota(jnp.int32, plan.tile, 1)
    return sub, lane


def row_parity():
    return lax.rem(lax.rem(lax.axis_index("tile") + TY // 2, TY), 2)


def band_parity():
    return lax.rem(lax.axis_index("band"), 2)


def level_speed(plan, bands, offset):
    band = lax.axis_index("band")
    speed = jnp.float32(0.7 * 1.1 ** -offset)
    for n in range(1, bands):
        speed = jnp.where(band == n, jnp.float32(0.7 * 1.1 ** -(n * plan.bins + offset)), speed)
    return speed


def lane_weights(plan):
    _, lane = iotas(plan)
    index = lax.rem(lax.rem(lane, plan.nd) // 2, plan.quad)
    cosine = sine = jnp.zeros(plan.tile, f32)
    for i in range(plan.quad):
        cosine = jnp.where(index == i, float(plan.cosines[i]), cosine)
        sine = jnp.where(index == i, float(plan.sines[i]), sine)
    return cosine, sine


def fill_weights(plan, bands, weight_ref):
    sub, _ = iotas(plan)
    for t in range(plan.weight_tiles):
        slope = rest = jnp.zeros(plan.tile, f32)
        for row in range(min(plan.rows, 3 * plan.quad - t * plan.rows)):
            i, c = divmod(t * plan.rows + row, 3)
            cosine, sine = float(plan.cosines[i]), float(plan.sines[i])
            slope = jnp.where(sub == row, (-cosine - sine, cosine, sine)[c], slope)
            rest = jnp.where(sub == row, 1.0 if c == 0 else 0.0, rest)
        for level in range(plan.levels):
            weight_ref[level, t] = rest + level_speed(plan, bands, level - FH) * slope


def spread(row, plan):
    return jnp.broadcast_to(row, plan.tile)


def pack_rows(plan, k, f_ref, g_ref, out_ref):
    sub, _ = iotas(plan)
    for sign in range(2):
        start = plan.rows - 2 if sign == 0 else 0
        for i in range(plan.quad):
            tiles = [ref[k, j] for j in plan.pair(sign, i) for ref in (f_ref, g_ref)]
            edge = rotate(tiles[3], 6 - start, 0)
            for n in (2, 1, 0):
                edge = jnp.where(sub < 2 * n + 2, rotate(tiles[n], 2 * n - start, 0), edge)
            out_ref[sign, k * plan.quad + i] = edge


def send_out(plan, f_ref, g_ref, rows_ref, row_refs, raw_refs):
    parity, band = row_parity(), band_parity()
    for n in range(2):
        towards = parity if n == 0 else 1 - parity
        row_refs[n][...] = rows_ref[towards]
        start = (band if n == 1 else 1 - band) * (plan.bins - FH)
        for field, ref in enumerate((f_ref, g_ref)):
            raw_refs[n][field] = ref[pl.ds(start, FH)]


def load_kernel(plan, bands, f_hbm, g_hbm, mask_ref, f_ref, g_ref, even_ref, odd_ref, raw_even, raw_odd, weight_ref, rows_ref, sems):
    mask = mask_ref[...].astype(f32)
    pairs = ((f_hbm, f_ref), (g_hbm, g_ref))
    copies = [
        [pltpu.make_async_copy(src.at[k], dst.at[k], sems.at[n, k]) for n, (src, dst) in enumerate(pairs)]
        for k in range(plan.bins)
    ]
    for level in copies:
        for copy in level:
            copy.start()
    fill_weights(plan, bands, weight_ref)
    for sign in range(2):
        rows_ref[sign, plan.last] = mask
    for k in range(plan.bins):
        for copy in copies[k]:
            copy.wait()

        def clear(j, _):
            f_ref[k, j] = f_ref[k, j] * mask
            g_ref[k, j] = g_ref[k, j] * mask
            return 0

        lax.fori_loop(0, plan.nd, clear, 0, unroll=12)
    lax.fori_loop(0, plan.bins, lambda k, _: pack_rows(plan, k, f_ref, g_ref, rows_ref) or 0, 0)
    send_out(plan, f_ref, g_ref, rows_ref, (even_ref, odd_ref), (raw_even, raw_odd))


def pack_kernel(plan, f_ref, g_ref, mask_ref, col_ref, even_ref, odd_ref):
    mask = mask_ref[...].astype(f32)
    _, lane = iotas(plan)
    pair_lane = lane // 2
    rows, lanes = plan.tile
    upward = row_parity() == 0
    for side in range(2):
        col_ref[side, 2 * plan.groups] = mask

    def part(at, _):
        packed = [[jnp.zeros(plan.tile, f32) for _ in range(2)] for _ in range(2)]
        for n in range(plan.group):
            for sign, i, side, j, field, _ in plan.tiles():
                slot = n * plan.half + sign * plan.quad + i
                shift = 2 * slot - (lanes - 2 if side == 0 else 0)
                value = rotate((f_ref, g_ref)[field][at * plan.group + n, j], shift, 1)
                packed[side][field] = jnp.where(pair_lane == slot, value, packed[side][field])
        for side in range(2):
            for field in range(2):
                where = field * plan.groups + at
                value = packed[side][field]
                col_ref[side, where] = value
                top, bottom = value[rows - 1 : rows], value[0:1]
                even_ref[side, pl.ds(where, 1), :] = jnp.where(upward, top, bottom)
                odd_ref[side, pl.ds(where, 1), :] = jnp.where(upward, bottom, top)
        return 0

    lax.fori_loop(0, plan.groups, part, 0)


def forward_kernel(plan, even_ref, odd_ref, col_ref, corner_even, corner_odd, rows_ref, corner_ref, fwd_even, fwd_odd):
    parity, band = row_parity(), band_parity()
    rows_ref[1 - parity] = even_ref[...]
    rows_ref[parity] = odd_ref[...]
    corner_ref[1 - parity] = corner_even[...]
    corner_ref[parity] = corner_odd[...]
    for n, out in enumerate((fwd_even, fwd_odd)):
        top = band if n == 1 else 1 - band
        part = top * (plan.groups - 1)
        start = top * (plan.bins - FH) * plan.quad
        for sign in range(2):
            out[sign * plan.sent_rows : (sign + 1) * plan.sent_rows] = rows_ref[sign, pl.ds(start, plan.sent_rows)]
            for side in range(2):
                for field in range(2):
                    row = 4 * sign + 2 * side + field
                    at = field * plan.groups + part
                    out[plan.sent - 1, row : row + 1, :] = corner_ref[sign, side, pl.ds(at, 1), :]
                    out[2 * plan.sent_rows + 2 * side + field] = col_ref[side, at]


def side_columns(plan, speeds, sides, lane_table, here_at, corner_at, out_at):
    sub, lane = iotas(plan)
    rows, _ = plan.tile
    in_group = lane // plan.nd
    odd = lane % 2 == 1
    northward = (lane % plan.nd) // 2 < plan.quad
    speed = jnp.where(in_group == 0, speeds[0], jnp.where(in_group == 1, speeds[1], speeds[2]))
    ua, va = (speed * weight for weight in lane_table)
    stay = 1.0 - ua - va
    for side in range(2):
        near, corner_masks = sides[side]
        for field in range(2):
            here = here_at(side, field)
            below, above = (spread(corner_at(sign, side, field), plan) for sign in range(2))
            across = rotate(here, 1 if side == 0 else -1, 1)
            along = jnp.where(
                northward,
                jnp.where(sub == 0, below, rotate(here, 1, 0)),
                jnp.where(sub == rows - 1, above, rotate(here, -1, 0)),
            )
            after = near * (stay * here + ua * across + va * along)
            corner = jnp.where(northward, corner_masks[0] * below, corner_masks[1] * above)
            after = after + va * corner
            if side == 0:
                out_at(side, field, jnp.where(odd, here, rotate(after, -1, 1)))
            else:
                out_at(side, field, jnp.where(odd, rotate(after, 1, 1), here))


def side_masks(plan, row_masks, col_ref):
    sub, _ = iotas(plan)
    rows, lanes = plan.tile
    sides = []
    for side in range(2):
        edge = lanes - 1 if side == 0 else 0
        own = lanes - 1 - edge
        near = spread(col_ref[side, 2 * plan.groups, :, edge : edge + 1], plan)
        corners = [
            jnp.where(sub == (0, rows - 1)[sign], spread(row_masks[sign][0:1, own : own + 1], plan), 0.0)
            for sign in range(2)
        ]
        sides.append((near, corners))
    return sides


def sweep(plan, count, mask, row_masks, weight_at, field_at, halo_at, column_at, store, scratch):
    rows_after, *rest = scratch
    columns_ref, first_ref, after_ref, second_ref = (rest[n * STAGES : (n + 1) * STAGES] for n in range(4))
    sub, lane = iotas(plan)
    rows, lanes = plan.tile
    first_half = sub < rows // 2
    outer = (first_half & (lane == 0)) | (~first_half & (lane == lanes - 1))
    edge_row, step_row = (0, rows - 1), (1, -1)
    near_lane, into = (0, lanes - 1), (1, -1)

    def weights(k, i):
        return [spread(weight_at(k, *divmod(3 * i + c, rows)), plan) for c in range(3)]

    def beside(x, halo, sign, side, field):
        inner = 4 * side + 2 * field + 1 - sign
        return jnp.where(sub == edge_row[sign], spread(halo(inner), plan), rotate(x, step_row[sign], 0))

    def gather(k, slot):
        columns = [[column_at(k, side, field) for field in range(2)] for side in range(2)]
        for sign, i, side, j, field, at in plan.tiles():
            lane_at = 2 * (sign * plan.quad + i)
            shift = -(lane_at + 1) if side == 0 else lanes - 1 - lane_at
            column = rotate(columns[side][field], shift, 1)
            columns_ref[slot][at] = column
            moved = rotate(field_at(field, k, j), into[side], 1)
            first_ref[slot][at] = jnp.where(lane == near_lane[side], column, moved)
        for i in range(plan.quad):
            stay, u, v = weights(k, i)
            for sign in range(2):
                halo = halo_at(sign, k, i)[...]
                across = jnp.where(first_half, rotate(halo, 1, 1), rotate(halo, -1, 1))
                across = jnp.where(outer, 0.0, across)
                along = rotate(halo, step_row[sign], 0)
                rows_after[sign, k * plan.quad + i] = row_masks[sign] * (stay * halo + u * across + v * along)

    def first(k, slot):
        for sign, i, side, j, field, at in plan.tiles():
            stay, u, v = weights(k, i)
            x = field_at(field, k, j)
            halo = halo_at(sign, k, i)
            y = beside(x, lambda n: halo[n : n + 1, :], sign, side, field)
            x = mask * (stay * x + u * first_ref[slot][at] + v * y)
            after_ref[slot][at] = x
            far = lanes - 1 - near_lane[side]
            second_ref[slot][at] = rotate(jnp.where(lane == far, columns_ref[slot][at], x), into[side], 1)

    def second(k, slot):
        for sign, i, side, j, field, at in plan.tiles():
            stay, u, v = weights(k, i)
            x = after_ref[slot][at]
            halo = rows_after.at[sign, k * plan.quad + i]
            y = beside(x, lambda n: halo[n : n + 1, :], sign, side, field)
            store(field, k, j, mask * (stay * x + u * second_ref[slot][at] + v * y))

    def clamp(k):
        return jnp.clip(k, 0, count - 1)

    def turn(t, _):
        for n in range(STAGES):
            at = t * STAGES + n
            second(clamp(at - 2), (n - 2) % STAGES)
            first(clamp(at - 1), (n - 1) % STAGES)
            gather(clamp(at), n)
        return 0

    lax.fori_loop(0, -(-(count + 2) // STAGES), turn, 0)


def sweep_scratch(plan, count):
    return [pltpu.VMEM((2, count * plan.quad) + plan.tile, f32)] + [
        pltpu.VMEM((2 * plan.nd,) + plan.tile, f32)
    ] * (4 * STAGES)


def halo_masks(plan, rows_ref):
    rows = plan.rows
    return [spread(rows_ref[0, plan.last, rows - 1 : rows, :], plan), spread(rows_ref[1, plan.last, 0:1, :], plan)]


def turned(plan, tile, place):
    back = lax.rem(plan.lanes - place * plan.nd, plan.lanes)
    return pltpu.roll(tile, back, 1)


def own_kernel(plan, bands, f_ref, g_ref, mask_ref, rows_ref, col_ref, corner_ref, weight_ref, ext_ref, both_ref, *scratch):
    row_masks = halo_masks(plan, rows_ref)
    sides = side_masks(plan, row_masks, col_ref)
    lane_table = lane_weights(plan)
    for part in range(plan.groups):

        def put(side, field, value):
            both_ref[side, field, part] = value

        side_columns(
            plan, [level_speed(plan, bands, part * plan.group + n) for n in range(plan.group)], sides, lane_table,
            lambda side, field: col_ref[side, field * plan.groups + part],
            lambda sign, side, field: corner_ref[sign, side, pl.ds(field * plan.groups + part, 1), :],
            put,
        )

    def store(field, k, j, value):
        ext_ref[field, (FH + k) * plan.nd + j] = value

    sweep(
        plan, plan.bins, mask_ref[...].astype(f32), row_masks,
        lambda k, t, row: weight_ref[FH + k, t, row : row + 1, :],
        lambda field, k, j: (f_ref, g_ref)[field][k, j],
        lambda sign, k, i: rows_ref.at[sign, k * plan.quad + i],
        lambda k, side, field: turned(plan, both_ref[side, field, lax.div(k, plan.group)], lax.rem(k, plan.group)),
        store, scratch,
    )


def halo_kernel(
    plan, bands, raw_even, raw_odd, fwd_even, fwd_odd, mask_ref, rows_ref, col_ref, weight_ref, ext_in,
    ext_ref, raw_ref, fwd_ref, both_ref, *scratch,
):
    band = band_parity()
    for field in range(2):
        raw_ref[field, pl.ds((1 - band) * FH, FH)] = raw_even[field]
        raw_ref[field, pl.ds(band * FH, FH)] = raw_odd[field]
    fwd_ref[1 - band] = fwd_even[...]
    fwd_ref[band] = fwd_odd[...]
    row_masks = halo_masks(plan, rows_ref)
    sides = side_masks(plan, row_masks, col_ref)
    lane_table = lane_weights(plan)
    for part in range(2):

        def put(side, field, value):
            both_ref[side, field, part] = value

        def corner(sign, side, field):
            row = 4 * sign + 2 * side + field
            return fwd_ref[part, plan.sent - 1, row : row + 1, :]

        side_columns(
            plan, [level_speed(plan, bands, part * (FH + plan.bins) - FH + n) for n in range(plan.group)], sides, lane_table,
            lambda side, field: fwd_ref[part, 2 * plan.sent_rows + 2 * side + field],
            corner,
            put,
        )

    def level(k):
        return jnp.where(k < FH, k, k + plan.bins)

    def store(field, k, j, value):
        ext_ref[field, level(k) * plan.nd + j] = value

    def halo(sign, k, i):
        part = jnp.where(k < FH, 0, 1)
        return fwd_ref.at[part, sign * plan.sent_rows + (k - part * FH) * plan.quad + i]

    def column(k, side, field):
        part = jnp.where(k < FH, 0, 1)
        return turned(plan, both_ref[side, field, part], k - part * FH)

    sweep(
        plan, 2 * FH, mask_ref[...].astype(f32), row_masks,
        lambda k, t, row: weight_ref[level(k), t, row : row + 1, :],
        lambda field, k, j: raw_ref[field, k, j],
        halo, column, store, scratch,
    )


def source_levels(plan, freq_ref, dir_ref, coupling_ref, ext_ref, fo_ref, go_ref, first, last):
    bins, nd = plan.bins, plan.nd
    p, q = freq_ref[0], freq_ref[1]
    e, h = dir_ref[0], dir_ref[1]
    span = (bins - 1) * nd + 1

    def wrap(j):
        return jnp.where(j >= nd, j - nd, jnp.where(j < 0, j + nd, j))

    def direction(j, _):
        def at(field, level, where):
            return ext_ref.at[field, pl.ds(level * nd + where, span)]

        own = [at(field, FH, j) for field in range(2)]
        up_one = [at(field, FH + p, wrap(j + e)) for field in range(2)]
        up_two = [at(field, FH + p, wrap(j - e)) for field in range(2)]
        low_one = [at(field, FH - q, wrap(j - h)) for field in range(2)]
        low_two = [at(field, FH - q, wrap(j + h)) for field in range(2)]
        out_f, out_g = (ref.at[pl.ds(j, span)] for ref in (fo_ref, go_ref))
        for k in range(bins):
            n = k * nd
            strength = source_step * coupling_ref[k]
            f0, g0 = own[0][n], own[1][n]
            fp1, gp1 = up_one[0][n], up_one[1][n]
            fp2, gp2 = up_two[0][n], up_two[1][n]
            fm1, gm1 = low_one[0][n], low_one[1][n]
            fm2, gm2 = low_two[0][n], low_two[1][n]
            linear = weight_plus * (fp1 + fp2) + weight_minus * (fm1 + fm2)
            linear_t = weight_plus * (gp1 + gp2) + weight_minus * (gm1 + gm2)
            cross = weight_cross * (fp1 * fm1 + fp2 * fm2)
            cross_t = weight_cross * ((gp1 * fm1 + fp1 * gm1) + (gp2 * fm2 + fp2 * gm2))
            f0l = f0 * linear
            both = f0l - cross
            rate = f0 * both
            change = g0 * (f0l + both) + f0 * (f0 * linear_t - cross_t)
            out_f[n] = f0 - strength * rate
            out_g[n] = g0 - strength * change
        return 0

    lax.fori_loop(first, last, direction, 0)


def flat(plan, ref):
    return ref.reshape((plan.bins * plan.nd,) + plan.tile)


def source_kernel(plan, freq_ref, dir_ref, coupling_ref, ext_ref, mask_ref, f_ref, g_ref, even_ref, odd_ref, raw_even, raw_odd, rows_ref):
    source_levels(plan, freq_ref, dir_ref, coupling_ref, ext_ref, flat(plan, f_ref), flat(plan, g_ref), 0, plan.nd)
    for sign in range(2):
        rows_ref[sign, plan.last] = mask_ref[...].astype(f32)
    lax.fori_loop(0, plan.bins, lambda k, _: pack_rows(plan, k, f_ref, g_ref, rows_ref) or 0, 0)
    send_out(plan, f_ref, g_ref, rows_ref, (even_ref, odd_ref), (raw_even, raw_odd))


def last_kernel(plan, chunks, freq_ref, dir_ref, coupling_ref, ext_ref, f_hbm, g_hbm, f_ref, g_ref, sems):
    each = plan.nd // chunks
    copies = []
    for n in range(chunks):
        source_levels(
            plan, freq_ref, dir_ref, coupling_ref, ext_ref, flat(plan, f_ref), flat(plan, g_ref), n * each, (n + 1) * each
        )
        part = pl.ds(n * each, each)
        for field, (src, dst) in enumerate(((f_ref, f_hbm), (g_ref, g_hbm))):
            copies.append(pltpu.make_async_copy(src.at[:, part], dst.at[:, part], sems.at[field, n]))
            copies[-1].start()
    for copy in copies:
        copy.wait()


def body(background, tangent, sea_mask, coupling, freq_offsets, dir_offsets):
    bins, nd = background.shape[:2]
    rows, lanes = background.shape[-2:]
    plan = Plan(bins, nd, rows, lanes)
    f = pltpu.with_memory_space_constraint(background.reshape(bins, nd, rows, lanes), pltpu.HBM)
    g = pltpu.with_memory_space_constraint(tangent.reshape(bins, nd, rows, lanes), pltpu.HBM)
    mask = sea_mask.reshape(rows, lanes)
    bands, tiles = lax.axis_size("band"), lax.axis_size("tile")

    def array(*shape):
        return jax.ShapeDtypeStruct(shape + plan.tile, f32)

    field = array(bins, nd)
    ext_out = array(2, plan.levels * nd)
    row_out = array(plan.last + 1)
    col_out = array(2, 2 * plan.groups + 1)
    corner_out = jax.ShapeDtypeStruct((2, -(-2 * plan.groups // 8) * 8, lanes), f32)
    raw_out = array(2, FH, nd)
    fwd_out = array(plan.sent)
    both = pltpu.VMEM((2, 2, plan.groups) + plan.tile, f32)
    sorted_rows = pltpu.VMEM((2, plan.last + 1) + plan.tile, f32)

    def kernel(function, out_shape, in_specs, scratch=(), out_specs=None, aliases={}, static=()):
        return pl.pallas_call(
            functools.partial(function, plan, *static),
            out_shape=out_shape,
            in_specs=in_specs,
            out_specs=out_specs or (VM,) * len(out_shape),
            scratch_shapes=list(scratch),
            input_output_aliases=aliases,
            compiler_params=pltpu.CompilerParams(vmem_limit_bytes=20 * 1024 * 1024),
        )

    def tile_pairs(parity, east):
        pairs = []
        for i in range(tiles):
            at = (i + TY // 2) % tiles
            row = at % TY
            if parity is not None:
                row += 1 if row % 2 == parity else -1
            if 0 <= row < TY:
                to = (at // TY * TY + row + east * TY) % tiles
                pairs.append((i, (to - TY // 2) % tiles))
        return pairs

    def tile_swap(value, parity):
        return lax.ppermute(value, "tile", tile_pairs(parity, 0))

    def sideways(value, parity):
        if tiles == 2 * TY:
            return lax.ppermute(value, "tile", tile_pairs(parity, 1))
        return jnp.concatenate(
            [lax.ppermute(value[n : n + 1], "tile", tile_pairs(parity, 1 - 2 * n)) for n in range(2)]
        )

    def band_swap(value, parity):
        pairs = [(i, i + 1 if i % 2 == parity else i - 1) for i in range(bands)]
        return lax.ppermute(value, "band", [(a, b) for a, b in pairs if 0 <= b < bands])

    f, g, even, odd, raw_even, raw_odd, weights = kernel(
        load_kernel,
        (field, field, row_out, row_out, raw_out, raw_out, array(plan.levels, plan.weight_tiles)),
        [HBM, HBM, VM],
        [sorted_rows, pltpu.SemaphoreType.DMA((2, bins))],
        static=(bands,),
    )(f, g, mask)

    for step in range(STEPS):
        odd = tile_swap(odd, 1)
        even = tile_swap(even, 0)
        raw_odd = band_swap(raw_odd, 1)
        raw_even = band_swap(raw_even, 0)
        cols, corner_even, corner_odd = kernel(pack_kernel, (col_out, corner_out, corner_out), [VM] * 3)(f, g, mask)
        cols = sideways(cols, None)
        corner_odd = sideways(corner_odd, 1)
        corner_even = sideways(corner_even, 0)
        sorted_out = (array(2, plan.last + 1), jax.ShapeDtypeStruct((2,) + corner_out.shape, f32), fwd_out, fwd_out)
        halo_rows, corners, fwd_even, fwd_odd = kernel(forward_kernel, sorted_out, [VM] * 5)(
            even, odd, cols, corner_even, corner_odd
        )
        fwd_odd = band_swap(fwd_odd, 1)
        fwd_even = band_swap(fwd_even, 0)
        (ext,) = kernel(
            own_kernel, (ext_out,), [VM] * 7, [both] + sweep_scratch(plan, bins), static=(bands,)
        )(f, g, mask, halo_rows, cols, corners, weights)
        (ext,) = kernel(
            halo_kernel,
            (ext_out,),
            [VM] * 9,
            [pltpu.VMEM((2, 2 * FH, nd) + plan.tile, f32), pltpu.VMEM((2, plan.sent) + plan.tile, f32), both]
            + sweep_scratch(plan, 2 * FH),
            aliases={8: 0},
            static=(bands,),
        )(raw_even, raw_odd, fwd_even, fwd_odd, mask, halo_rows, cols, weights, ext)
        if step < STEPS - 1:
            f, g, even, odd, raw_even, raw_odd = kernel(
                source_kernel, (field, field, row_out, row_out, raw_out, raw_out), [SM] * 3 + [VM] * 2, [sorted_rows]
            )(freq_offsets, dir_offsets, coupling, ext, mask)
        else:
            chunks = 6
            f, g = kernel(
                lambda plan, *refs: last_kernel(plan, chunks, *refs),
                (field, field),
                [SM] * 3 + [VM],
                [pltpu.VMEM(field.shape, f32)] * 2 + [pltpu.SemaphoreType.DMA((2, chunks))],
                out_specs=(HBM, HBM),
            )(freq_offsets, dir_offsets, coupling, ext)
    return f.reshape(background.shape), g.reshape(tangent.shape)


def solution(mesh):
    in_specs = (
        P("band", None, "tile", None, None),
        P("band", None, "tile", None, None),
        P("tile", None, None),
        P("band"),
        P(),
        P(),
    )
    out_specs = (P("band", None, "tile", None, None), P("band", None, "tile", None, None))
    return jax.shard_map(body, mesh=mesh, in_specs=in_specs, out_specs=out_specs, check_vma=False)
```

```python
import functools
import math

import jax
import jax.numpy as jnp
import numpy as np
from jax import lax
from jax.experimental import pallas as pl
from jax.experimental.pallas import tpu as pltpu
from jax.sharding import PartitionSpec as P


TY = 4
FH = 3
STEPS = 2

weight_plus = 1.0 / 1.25**4
weight_minus = 1.0 / 0.75**4
weight_cross = 1.0 / (1.0 - 0.25**2) ** 4
source_step = 0.5

VM = pl.BlockSpec(memory_space=pltpu.VMEM)
SM = pl.BlockSpec(memory_space=pltpu.SMEM)
HBM = pl.BlockSpec(memory_space=pltpu.HBM)
f32 = jnp.float32


def rotate(x, shift, axis):
    shift = shift % x.shape[axis]
    return x if shift == 0 else pltpu.roll(x, shift, axis)


class Plan:
    def __init__(self, bins, nd, rows, lanes):
        self.bins, self.nd, self.rows, self.lanes = bins, nd, rows, lanes
        self.half, self.quad = nd // 2, nd // 4
        self.group = lanes // nd
        self.groups = bins // self.group
        assert self.group == FH and bins == FH * self.groups and nd == 4 * self.quad and bins >= 2 * FH
        angles = (np.arange(self.quad) + 0.5) * (2.0 * math.pi / nd)
        self.cosines, self.sines = np.cos(angles), np.sin(angles)
        self.tile = (rows, lanes)
        self.levels = bins + 2 * FH
        self.last = bins * self.quad
        self.weight_tiles = -(-3 * self.quad // rows)
        self.sent_rows = FH * self.quad
        self.sent = 2 * self.sent_rows + 5

    def pair(self, sign, i):
        return (i, self.half - 1 - i) if sign == 0 else (self.nd - 1 - i, self.half + i)

    def tiles(self, sign):
        for i in range(self.quad):
            for side, j in enumerate(self.pair(sign, i)):
                for field in range(2):
                    yield i, side, j, field, 4 * i + 2 * side + field


def iotas(plan):
    sub = lax.broadcasted_iota(jnp.int32, plan.tile, 0)
    lane = lax.broadcasted_iota(jnp.int32, plan.tile, 1)
    return sub, lane


def row_parity():
    return lax.rem(lax.rem(lax.axis_index("tile") + TY // 2, TY), 2)


def band_parity():
    return lax.rem(lax.axis_index("band"), 2)


def level_speed(plan, bands, offset):
    band = lax.axis_index("band")
    speed = jnp.float32(0.7 * 1.1 ** -offset)
    for n in range(1, bands):
        speed = jnp.where(band == n, jnp.float32(0.7 * 1.1 ** -(n * plan.bins + offset)), speed)
    return speed


def lane_weights(plan):
    _, lane = iotas(plan)
    index = lax.rem(lax.rem(lane, plan.nd) // 2, plan.quad)
    cosine = sine = jnp.zeros(plan.tile, f32)
    for i in range(plan.quad):
        cosine = jnp.where(index == i, float(plan.cosines[i]), cosine)
        sine = jnp.where(index == i, float(plan.sines[i]), sine)
    return cosine, sine


def fill_weights(plan, bands, weight_ref):
    sub, _ = iotas(plan)
    for t in range(plan.weight_tiles):
        slope = rest = jnp.zeros(plan.tile, f32)
        for row in range(min(plan.rows, 3 * plan.quad - t * plan.rows)):
            i, c = divmod(t * plan.rows + row, 3)
            cosine, sine = float(plan.cosines[i]), float(plan.sines[i])
            slope = jnp.where(sub == row, (-cosine - sine, cosine, sine)[c], slope)
            rest = jnp.where(sub == row, 1.0 if c == 0 else 0.0, rest)
        for level in range(plan.levels):
            weight_ref[level, t] = rest + level_speed(plan, bands, level - FH) * slope


def spread(row, plan):
    return jnp.broadcast_to(row, plan.tile)


def pack_rows(plan, k, f_ref, g_ref, out_ref):
    sub, _ = iotas(plan)
    for sign in range(2):
        start = plan.rows - 2 if sign == 0 else 0
        for i in range(plan.quad):
            tiles = [ref[k, j] for j in plan.pair(sign, i) for ref in (f_ref, g_ref)]
            edge = rotate(tiles[3], 6 - start, 0)
            for n in (2, 1, 0):
                edge = jnp.where(sub < 2 * n + 2, rotate(tiles[n], 2 * n - start, 0), edge)
            out_ref[sign, k * plan.quad + i] = edge


def send_out(plan, f_ref, g_ref, rows_ref, row_refs, raw_refs):
    parity, band = row_parity(), band_parity()
    for n in range(2):
        towards = parity if n == 0 else 1 - parity
        row_refs[n][...] = rows_ref[towards]
        start = (band if n == 1 else 1 - band) * (plan.bins - FH)
        for field, ref in enumerate((f_ref, g_ref)):
            raw_refs[n][field] = ref[pl.ds(start, FH)]


def load_kernel(plan, bands, f_hbm, g_hbm, mask_ref, f_ref, g_ref, even_ref, odd_ref, raw_even, raw_odd, weight_ref, rows_ref, sems):
    mask = mask_ref[...].astype(f32)
    pairs = ((f_hbm, f_ref), (g_hbm, g_ref))
    copies = [
        [pltpu.make_async_copy(src.at[k], dst.at[k], sems.at[n, k]) for n, (src, dst) in enumerate(pairs)]
        for k in range(plan.bins)
    ]
    for level in copies:
        for copy in level:
            copy.start()
    fill_weights(plan, bands, weight_ref)
    for sign in range(2):
        rows_ref[sign, plan.last] = mask
    for k in range(plan.bins):
        for copy in copies[k]:
            copy.wait()

        def clear(j, _):
            f_ref[k, j] = f_ref[k, j] * mask
            g_ref[k, j] = g_ref[k, j] * mask
            return 0

        lax.fori_loop(0, plan.nd, clear, 0, unroll=12)
    lax.fori_loop(0, plan.bins, lambda k, _: pack_rows(plan, k, f_ref, g_ref, rows_ref) or 0, 0)
    send_out(plan, f_ref, g_ref, rows_ref, (even_ref, odd_ref), (raw_even, raw_odd))


def pack_kernel(plan, f_ref, g_ref, mask_ref, col_ref, even_ref, odd_ref):
    mask = mask_ref[...].astype(f32)
    _, lane = iotas(plan)
    pair_lane = lane // 2
    rows, lanes = plan.tile
    upward = row_parity() == 0
    for side in range(2):
        col_ref[side, 2 * plan.groups] = mask

    def part(at, _):
        packed = [[jnp.zeros(plan.tile, f32) for _ in range(2)] for _ in range(2)]
        for n in range(plan.group):
            for sign in range(2):
                for i, side, j, field, _ in plan.tiles(sign):
                    slot = n * plan.half + sign * plan.quad + i
                    shift = 2 * slot - (lanes - 2 if side == 0 else 0)
                    value = rotate((f_ref, g_ref)[field][at * plan.group + n, j], shift, 1)
                    packed[side][field] = jnp.where(pair_lane == slot, value, packed[side][field])
        for side in range(2):
            for field in range(2):
                where = field * plan.groups + at
                value = packed[side][field]
                col_ref[side, where] = value
                top, bottom = value[rows - 1 : rows], value[0:1]
                even_ref[side, pl.ds(where, 1), :] = jnp.where(upward, top, bottom)
                odd_ref[side, pl.ds(where, 1), :] = jnp.where(upward, bottom, top)
        return 0

    lax.fori_loop(0, plan.groups, part, 0)


def forward_kernel(plan, even_ref, odd_ref, col_ref, corner_even, corner_odd, rows_ref, corner_ref, fwd_even, fwd_odd):
    parity, band = row_parity(), band_parity()
    rows_ref[1 - parity] = even_ref[...]
    rows_ref[parity] = odd_ref[...]
    corner_ref[1 - parity] = corner_even[...]
    corner_ref[parity] = corner_odd[...]
    for n, out in enumerate((fwd_even, fwd_odd)):
        top = band if n == 1 else 1 - band
        part = top * (plan.groups - 1)
        start = top * (plan.bins - FH) * plan.quad
        for sign in range(2):
            out[sign * plan.sent_rows : (sign + 1) * plan.sent_rows] = rows_ref[sign, pl.ds(start, plan.sent_rows)]
            for side in range(2):
                for field in range(2):
                    row = 4 * sign + 2 * side + field
                    at = field * plan.groups + part
                    out[plan.sent - 1, row : row + 1, :] = corner_ref[sign, side, pl.ds(at, 1), :]
                    out[2 * plan.sent_rows + 2 * side + field] = col_ref[side, at]


def side_columns(plan, speeds, sides, lane_table, here_at, corner_at, out_at):
    sub, lane = iotas(plan)
    rows, _ = plan.tile
    in_group = lane // plan.nd
    odd = lane % 2 == 1
    northward = (lane % plan.nd) // 2 < plan.quad
    speed = jnp.where(in_group == 0, speeds[0], jnp.where(in_group == 1, speeds[1], speeds[2]))
    ua, va = (speed * weight for weight in lane_table)
    stay = 1.0 - ua - va

    def along(x, below, above):
        return jnp.where(
            northward,
            jnp.where(sub == 0, below, rotate(x, 1, 0)),
            jnp.where(sub == rows - 1, above, rotate(x, -1, 0)),
        )

    for side in range(2):
        near, own, inner, corner_masks = sides[side]
        for field in range(2):
            here = here_at(side, field)
            below, above = (spread(corner_at(sign, side, field), plan) for sign in range(2))
            across = rotate(here, 1 if side == 0 else -1, 1)
            after = near * (stay * here + ua * across + va * along(here, below, above))
            after = after + va * jnp.where(northward, corner_masks[0] * below, corner_masks[1] * above)
            once = own * (ua * here)
            outer = own * (stay * once + ua * after + va * along(once, 0.0, 0.0))
            second = inner * (ua * once)
            if side == 0:
                out_at(side, field, jnp.where(odd, second, rotate(outer, -1, 1)))
            else:
                out_at(side, field, jnp.where(odd, rotate(outer, 1, 1), second))


def side_masks(plan, mask_ref, row_masks, col_ref):
    sub, _ = iotas(plan)
    rows, lanes = plan.tile
    sides = []
    for side in range(2):
        edge = lanes - 1 if side == 0 else 0
        own = lanes - 1 - edge
        near = spread(col_ref[side, 2 * plan.groups, :, edge : edge + 1], plan)
        corners = [
            jnp.where(sub == (0, rows - 1)[sign], spread(row_masks[sign][0:1, own : own + 1], plan), 0.0)
            for sign in range(2)
        ]
        mine = [
            spread(mask_ref[:, at : at + 1].astype(f32), plan) for at in (own, own + (1 if side == 0 else -1))
        ]
        sides.append((near, *mine, corners))
    return sides


INTO = (1, -1)


def weights(plan, weight_ref, level, i):
    return [spread(weight_ref[level, t, row : row + 1, :], plan) for t, row in (divmod(3 * i + c, plan.rows) for c in range(3))]


def inside(plan, count, mask, weight_ref, level_of, field_at, ext_ref, scratch):
    moved_ref, after_ref, second_ref = (scratch[2 * n : 2 * n + 2] for n in range(3))
    sub, lane = iotas(plan)
    rows, lanes = plan.tile
    edge_row, step_row, near_lane = (0, rows - 1), (1, -1), (0, lanes - 1)

    def step(k, sign, value_at, moved_at):
        for i, side, j, field, at in plan.tiles(sign):
            stay, u, v = weights(plan, weight_ref, level_of(k), i)
            u = jnp.where(lane == near_lane[side], 0.0, u)
            v = jnp.where(sub == edge_row[sign], 0.0, v)
            x = value_at(i, side, j, field, at)
            yield side, j, field, at, mask * (stay * x + u * moved_at[at] + v * rotate(x, step_row[sign], 0))

    def gather(k, sign):
        for i, side, j, field, at in plan.tiles(sign):
            moved_ref[sign][at] = rotate(field_at(field, k, j), INTO[side], 1)

    def first(k, sign):
        for side, j, field, at, x in step(k, sign, lambda i, side, j, field, at: field_at(field, k, j), moved_ref[sign]):
            after_ref[sign][at] = x
            second_ref[sign][at] = rotate(x, INTO[side], 1)

    def second(k, sign):
        for side, j, field, at, x in step(k, sign, lambda i, side, j, field, at: after_ref[sign][at], second_ref[sign]):
            ext_ref[field, level_of(k) * plan.nd + j] = x

    def turn(k, _):
        before, here = jnp.maximum(k - 1, 0), jnp.minimum(k, count - 1)
        second(before, 0)
        first(before, 1)
        gather(here, 0)
        second(before, 1)
        first(here, 0)
        gather(here, 1)
        return 0

    lax.fori_loop(0, count + 1, turn, 0)


def add_edges(plan, levels, mask_ref, row_masks, weight_ref, level_of, halo_at, column_at, ext_ref):
    sub, lane = iotas(plan)
    rows, lanes = plan.tile
    first_half = sub < rows // 2
    outer = (first_half & (lane == 0)) | (~first_half & (lane == lanes - 1))
    odd = sub % 2 == 1

    def sideways(x):
        return jnp.where(outer, 0.0, jnp.where(first_half, rotate(x, 1, 1), rotate(x, -1, 1)))

    edge, inner, beside = [], [], []
    for sign in range(2):
        at = 0 if sign == 0 else rows - 1
        step = 1 if sign == 0 else -1
        edge.append(spread(mask_ref[at : at + 1, :].astype(f32), plan))
        inner.append(spread(mask_ref[at + step : at + step + 1, :].astype(f32), plan))
        beside.append(sideways(edge[sign]))
    for k in levels:
        level = level_of(k)
        columns = [[column_at(k, side, field) for field in range(2)] for side in range(2)]
        for sign in range(2):
            place = odd if sign == 0 else ~odd
            for i in range(plan.quad):
                stay, u, v = weights(plan, weight_ref, level, i)
                halo = halo_at(sign, k, i)
                nearest = jnp.where(place, halo, rotate(halo, -1 if sign == 0 else 1, 0))
                shifted = sideways(nearest)
                after = row_masks[sign] * (stay * nearest + u * shifted + v * halo)
                once = edge[sign] * (v * nearest)
                new = edge[sign] * (stay * once + u * (v * (beside[sign] * shifted)) + v * after)
                new = jnp.where(place, inner[sign] * (v * once), new)
                for side, j in enumerate(plan.pair(sign, i)):
                    for field in range(2):
                        n = 4 * side + 2 * field
                        row_part = rotate(new, -n if sign == 0 else rows - 2 - n, 0)
                        row_here = sub < 2 if sign == 0 else sub >= rows - 2
                        slot = 2 * (sign * plan.quad + i)
                        column = rotate(columns[side][field], -slot if side == 0 else lanes - 2 - slot, 1)
                        lane_here = lane < 2 if side == 0 else lane >= lanes - 2
                        at = level * plan.nd + j
                        x = ext_ref[field, at]
                        x = x + jnp.where(row_here, row_part, 0.0)
                        ext_ref[field, at] = x + jnp.where(lane_here, column, 0.0)


def half_scratch(plan):
    return [pltpu.VMEM((plan.nd,) + plan.tile, f32)] * 6


def halo_masks(plan, rows_ref):
    rows = plan.rows
    return [spread(rows_ref[0, plan.last, rows - 1 : rows, :], plan), spread(rows_ref[1, plan.last, 0:1, :], plan)]


def own_kernel(plan, f_ref, g_ref, mask_ref, weight_ref, ext_ref, *scratch):
    mask = mask_ref[...].astype(f32)
    inside(
        plan, plan.bins, mask, weight_ref, lambda k: FH + k, lambda field, k, j: (f_ref, g_ref)[field][k, j],
        ext_ref, scratch,
    )


def own_edges_kernel(plan, bands, mask_ref, rows_ref, col_ref, corner_ref, weight_ref, ext_in, ext_ref, column_ref):
    row_masks = halo_masks(plan, rows_ref)
    sides = side_masks(plan, mask_ref, row_masks, col_ref)
    lane_table = lane_weights(plan)
    for part in range(plan.groups):

        def put(side, field, value):
            column_ref[side, field, part] = value

        side_columns(
            plan, [level_speed(plan, bands, part * plan.group + n) for n in range(plan.group)], sides, lane_table,
            lambda side, field: col_ref[side, field * plan.groups + part],
            lambda sign, side, field: corner_ref[sign, side, pl.ds(field * plan.groups + part, 1), :],
            put,
        )

    def part(at, _):
        add_edges(
            plan, range(plan.group), mask_ref, row_masks, weight_ref,
            lambda n: FH + at * plan.group + n,
            lambda sign, n, i: rows_ref[sign, (at * plan.group + n) * plan.quad + i],
            lambda n, side, field: rotate(column_ref[side, field, at], -n * plan.nd, 1),
            ext_ref,
        )
        return 0

    lax.fori_loop(0, plan.groups, part, 0)


def halo_kernel(plan, raw_even, raw_odd, mask_ref, weight_ref, ext_in, ext_ref, *scratch):
    band = band_parity()
    mask = mask_ref[...].astype(f32)
    for above, ref in ((1 - band, raw_even), (band, raw_odd)):
        start = above * (FH + plan.bins)
        inside(
            plan, FH, mask, weight_ref, lambda k: start + k, lambda field, k, j: ref[field, k, j], ext_ref, scratch
        )


def halo_edges_kernel(
    plan, bands, fwd_even, fwd_odd, mask_ref, rows_ref, col_ref, weight_ref, ext_in, ext_ref, fwd_ref, column_ref
):
    band = band_parity()
    fwd_ref[1 - band] = fwd_even[...]
    fwd_ref[band] = fwd_odd[...]
    row_masks = halo_masks(plan, rows_ref)
    sides = side_masks(plan, mask_ref, row_masks, col_ref)
    lane_table = lane_weights(plan)
    for part in range(2):

        def put(side, field, value):
            column_ref[side, field, part] = value

        def corner(sign, side, field):
            row = 4 * sign + 2 * side + field
            return fwd_ref[part, plan.sent - 1, row : row + 1, :]

        side_columns(
            plan, [level_speed(plan, bands, part * (FH + plan.bins) - FH + n) for n in range(plan.group)], sides, lane_table,
            lambda side, field: fwd_ref[part, 2 * plan.sent_rows + 2 * side + field],
            corner,
            put,
        )

    def part(at, _):
        add_edges(
            plan, range(FH), mask_ref, row_masks, weight_ref,
            lambda n: at * (FH + plan.bins) + n,
            lambda sign, n, i: fwd_ref[at, sign * plan.sent_rows + n * plan.quad + i],
            lambda n, side, field: rotate(column_ref[side, field, at], -n * plan.nd, 1),
            ext_ref,
        )
        return 0

    lax.fori_loop(0, 2, part, 0)


def source_levels(plan, freq_ref, dir_ref, coupling_ref, ext_ref, fo_ref, go_ref, first, last):
    bins, nd = plan.bins, plan.nd
    p, q = freq_ref[0], freq_ref[1]
    e, h = dir_ref[0], dir_ref[1]
    span = (bins - 1) * nd + 1

    def wrap(j):
        return jnp.where(j >= nd, j - nd, jnp.where(j < 0, j + nd, j))

    def direction(j, _):
        def at(field, level, where):
            return ext_ref.at[field, pl.ds(level * nd + where, span)]

        own = [at(field, FH, j) for field in range(2)]
        up_one = [at(field, FH + p, wrap(j + e)) for field in range(2)]
        up_two = [at(field, FH + p, wrap(j - e)) for field in range(2)]
        low_one = [at(field, FH - q, wrap(j - h)) for field in range(2)]
        low_two = [at(field, FH - q, wrap(j + h)) for field in range(2)]
        out_f, out_g = (ref.at[pl.ds(j, span)] for ref in (fo_ref, go_ref))
        for k in range(bins):
            n = k * nd
            strength = source_step * coupling_ref[k]
            f0, g0 = own[0][n], own[1][n]
            fp1, gp1 = up_one[0][n], up_one[1][n]
            fp2, gp2 = up_two[0][n], up_two[1][n]
            fm1, gm1 = low_one[0][n], low_one[1][n]
            fm2, gm2 = low_two[0][n], low_two[1][n]
            linear = weight_plus * (fp1 + fp2) + weight_minus * (fm1 + fm2)
            linear_t = weight_plus * (gp1 + gp2) + weight_minus * (gm1 + gm2)
            cross = weight_cross * (fp1 * fm1 + fp2 * fm2)
            cross_t = weight_cross * ((gp1 * fm1 + fp1 * gm1) + (gp2 * fm2 + fp2 * gm2))
            f0l = f0 * linear
            both = f0l - cross
            rate = f0 * both
            change = g0 * (f0l + both) + f0 * (f0 * linear_t - cross_t)
            out_f[n] = f0 - strength * rate
            out_g[n] = g0 - strength * change
        return 0

    lax.fori_loop(first, last, direction, 0, unroll=2)


def flat(plan, ref):
    return ref.reshape((plan.bins * plan.nd,) + plan.tile)


def source_kernel(plan, freq_ref, dir_ref, coupling_ref, ext_ref, mask_ref, f_ref, g_ref, even_ref, odd_ref, raw_even, raw_odd, rows_ref):
    source_levels(plan, freq_ref, dir_ref, coupling_ref, ext_ref, flat(plan, f_ref), flat(plan, g_ref), 0, plan.nd)
    for sign in range(2):
        rows_ref[sign, plan.last] = mask_ref[...].astype(f32)
    lax.fori_loop(0, plan.bins, lambda k, _: pack_rows(plan, k, f_ref, g_ref, rows_ref) or 0, 0)
    send_out(plan, f_ref, g_ref, rows_ref, (even_ref, odd_ref), (raw_even, raw_odd))


def last_kernel(plan, chunks, freq_ref, dir_ref, coupling_ref, ext_ref, f_hbm, g_hbm, f_ref, g_ref, sems):
    each = plan.nd // chunks
    copies = []
    for n in range(chunks):
        source_levels(
            plan, freq_ref, dir_ref, coupling_ref, ext_ref, flat(plan, f_ref), flat(plan, g_ref), n * each, (n + 1) * each
        )
        part = pl.ds(n * each, each)
        for field, (src, dst) in enumerate(((f_ref, f_hbm), (g_ref, g_hbm))):
            copies.append(pltpu.make_async_copy(src.at[:, part], dst.at[:, part], sems.at[field, n]))
            copies[-1].start()
    for copy in copies:
        copy.wait()


def body(background, tangent, sea_mask, coupling, freq_offsets, dir_offsets):
    bins, nd = background.shape[:2]
    rows, lanes = background.shape[-2:]
    plan = Plan(bins, nd, rows, lanes)
    f = pltpu.with_memory_space_constraint(background.reshape(bins, nd, rows, lanes), pltpu.HBM)
    g = pltpu.with_memory_space_constraint(tangent.reshape(bins, nd, rows, lanes), pltpu.HBM)
    mask = sea_mask.reshape(rows, lanes)
    bands, tiles = lax.axis_size("band"), lax.axis_size("tile")

    def array(*shape):
        return jax.ShapeDtypeStruct(shape + plan.tile, f32)

    field = array(bins, nd)
    ext_out = array(2, plan.levels * nd)
    row_out = array(plan.last + 1)
    col_out = array(2, 2 * plan.groups + 1)
    corner_out = jax.ShapeDtypeStruct((2, -(-2 * plan.groups // 8) * 8, lanes), f32)
    raw_out = array(2, FH, nd)
    fwd_out = array(plan.sent)
    both = pltpu.VMEM((2, 2, plan.groups) + plan.tile, f32)
    sorted_rows = pltpu.VMEM((2, plan.last + 1) + plan.tile, f32)

    def kernel(function, out_shape, in_specs, scratch=(), out_specs=None, aliases={}, static=()):
        return pl.pallas_call(
            functools.partial(function, plan, *static),
            out_shape=out_shape,
            in_specs=in_specs,
            out_specs=out_specs or (VM,) * len(out_shape),
            scratch_shapes=list(scratch),
            input_output_aliases=aliases,
            compiler_params=pltpu.CompilerParams(vmem_limit_bytes=20 * 1024 * 1024),
        )

    def tile_pairs(parity, east):
        pairs = []
        for i in range(tiles):
            at = (i + TY // 2) % tiles
            row = at % TY
            if parity is not None:
                row += 1 if row % 2 == parity else -1
            if 0 <= row < TY:
                to = (at // TY * TY + row + east * TY) % tiles
                pairs.append((i, (to - TY // 2) % tiles))
        return pairs

    def tile_swap(value, parity):
        return lax.ppermute(value, "tile", tile_pairs(parity, 0))

    def sideways(value, parity):
        if tiles == 2 * TY:
            return lax.ppermute(value, "tile", tile_pairs(parity, 1))
        return jnp.concatenate(
            [lax.ppermute(value[n : n + 1], "tile", tile_pairs(parity, 1 - 2 * n)) for n in range(2)]
        )

    def band_swap(value, parity):
        pairs = [(i, i + 1 if i % 2 == parity else i - 1) for i in range(bands)]
        return lax.ppermute(value, "band", [(a, b) for a, b in pairs if 0 <= b < bands])

    f, g, even, odd, raw_even, raw_odd, weights = kernel(
        load_kernel,
        (field, field, row_out, row_out, raw_out, raw_out, array(plan.levels, plan.weight_tiles)),
        [HBM, HBM, VM],
        [sorted_rows, pltpu.SemaphoreType.DMA((2, bins))],
        static=(bands,),
    )(f, g, mask)

    for step in range(STEPS):
        odd = tile_swap(odd, 1)
        even = tile_swap(even, 0)
        raw_odd = band_swap(raw_odd, 1)
        raw_even = band_swap(raw_even, 0)
        cols, corner_even, corner_odd = kernel(pack_kernel, (col_out, corner_out, corner_out), [VM] * 3)(f, g, mask)
        cols = sideways(cols, None)
        corner_odd = sideways(corner_odd, 1)
        corner_even = sideways(corner_even, 0)
        (ext,) = kernel(own_kernel, (ext_out,), [VM] * 4, half_scratch(plan))(f, g, mask, weights)
        sorted_out = (array(2, plan.last + 1), jax.ShapeDtypeStruct((2,) + corner_out.shape, f32), fwd_out, fwd_out)
        halo_rows, corners, fwd_even, fwd_odd = kernel(forward_kernel, sorted_out, [VM] * 5)(
            even, odd, cols, corner_even, corner_odd
        )
        fwd_odd = band_swap(fwd_odd, 1)
        fwd_even = band_swap(fwd_even, 0)
        (ext,) = kernel(
            own_edges_kernel, (ext_out,), [VM] * 6, [both], aliases={5: 0}, static=(bands,)
        )(mask, halo_rows, cols, corners, weights, ext)
        (ext,) = kernel(halo_kernel, (ext_out,), [VM] * 5, half_scratch(plan), aliases={4: 0})(
            raw_even, raw_odd, mask, weights, ext,
        )
        (ext,) = kernel(
            halo_edges_kernel,
            (ext_out,),
            [VM] * 7,
            [pltpu.VMEM((2, plan.sent) + plan.tile, f32), both],
            aliases={6: 0},
            static=(bands,),
        )(fwd_even, fwd_odd, mask, halo_rows, cols, weights, ext)
        if step < STEPS - 1:
            f, g, even, odd, raw_even, raw_odd = kernel(
                source_kernel, (field, field, row_out, row_out, raw_out, raw_out), [SM] * 3 + [VM] * 2, [sorted_rows]
            )(freq_offsets, dir_offsets, coupling, ext, mask)
        else:
            chunks = 6
            f, g = kernel(
                lambda plan, *refs: last_kernel(plan, chunks, *refs),
                (field, field),
                [SM] * 3 + [VM],
                [pltpu.VMEM(field.shape, f32)] * 2 + [pltpu.SemaphoreType.DMA((2, chunks))],
                out_specs=(HBM, HBM),
            )(freq_offsets, dir_offsets, coupling, ext)
    return f.reshape(background.shape), g.reshape(tangent.shape)


def solution(mesh):
    in_specs = (
        P("band", None, "tile", None, None),
        P("band", None, "tile", None, None),
        P("tile", None, None),
        P("band"),
        P(),
        P(),
    )
    out_specs = (P("band", None, "tile", None, None), P("band", None, "tile", None, None))
    return jax.shard_map(body, mesh=mesh, in_specs=in_specs, out_specs=out_specs, check_vma=False)
```
